32 devices in a mesh: seq: 4 (over y, core), fsdp: 8 (over z, x).
Axes of the slice: x: 2, y: 2, z: 4, core: 2. Of those that a mesh axis runs over, the one named last changes fastest.
Arguments:
- tokens: bfloat16 [8, 1024, 768], P('fsdp', 'seq'), may hold values from -6 to 6
- segment_ids: int32 [8, 1024], P('fsdp', 'seq'), may hold values from 0 to 3, never falling along the last dimension, each value on 1 to 512 neighbouring positions
- query_weight: bfloat16 [768, 768], P('fsdp'), may hold values from -0.4375 to 0.4375
- key_weight: bfloat16 [768, 768], P('fsdp'), may hold values from -0.21875 to 0.21875
- value_weight: bfloat16 [768, 768], P('fsdp'), may hold values from -0.21875 to 0.21875
- merge_weight: bfloat16 [768, 768], P('fsdp'), may hold values from -0.875 to 0.875
- query_bias: bfloat16 [768], P('fsdp'), may hold values from -3 to 3
- value_bias: bfloat16 [768], P('fsdp'), may hold values from -3 to 3
- merge_bias: bfloat16 [768], P('fsdp'), may hold values from -3 to 3
- first_gain: bfloat16 [768], P('fsdp'), may hold values from 0.5 to 1.5
- first_shift: bfloat16 [768], P('fsdp'), may hold values from -3 to 3
- expand_weight: bfloat16 [768, 3072], P('fsdp'), may hold values from -0.21875 to 0.21875
- expand_bias: bfloat16 [3072], P('fsdp'), may hold values from -3 to 3
- shrink_weight: bfloat16 [3072, 768], P('fsdp'), may hold values from -0.21875 to 0.21875
- shrink_bias: bfloat16 [768], P('fsdp'), may hold values from -3 to 3
- second_gain: bfloat16 [768], P('fsdp'), may hold values from 0.5 to 1.5
- second_shift: bfloat16 [768], P('fsdp'), may hold values from -3 to 3
- cotangent: bfloat16 [8, 1024, 768], P('fsdp', 'seq'), may hold values from -6 to 6
Outputs:
- output: bfloat16 [8, 1024, 768], P('fsdp', 'seq')
- input_grad: bfloat16 [8, 1024, 768], P('fsdp', 'seq')
- query_weight_grad: float32 [768, 768], P('fsdp')
- key_weight_grad: float32 [768, 768], P('fsdp')
- value_weight_grad: float32 [768, 768], P('fsdp')
- merge_weight_grad: float32 [768, 768], P('fsdp')
- query_bias_grad: float32 [768], P('fsdp')
- value_bias_grad: float32 [768], P('fsdp')
- merge_bias_grad: float32 [768], P('fsdp')
- first_gain_grad: float32 [768], P('fsdp')
- first_shift_grad: float32 [768], P('fsdp')
- expand_weight_grad: float32 [768, 3072], P('fsdp')
- expand_bias_grad: float32 [3072], P('fsdp')
- shrink_weight_grad: float32 [3072, 768], P('fsdp')
- shrink_bias_grad: float32 [768], P('fsdp')
- second_gain_grad: float32 [768], P('fsdp')
- second_shift_grad: float32 [768], P('fsdp')
The draws below stay inside these ranges and needn't reach their ends.
Inputs may be any that keep to these rules, and one draw needn't show every extreme that they name: `segment_ids`: in each sequence the ids never fall, every id appears, a document holds at most 512 tokens, and some document holds exactly that many.
All inputs are finite; a program needn't handle non-finite values.
Results may differ from the reference program's by a relative error of at most 0.019.
Values may be sent and summed in bfloat16 or wider, within the bound.
No kernel may reach another device: no remote copies, remote signals or barrier semaphores. Data moves between devices by JAX's collectives and lax.ppermute only.
A program may use at most 128 MiB of HBM per device.

```python
import math
import jax
import jax.numpy as jnp
import numpy as np
from jax import lax

D = 768
HEADS = 12
HEAD_DIM = 64
FF = 3072
DOCS = 4
LEN = 1024
SEQS = 8


def shard_levels(own_key, extent, cuts, least, high):
    def one(axis_at, shards_of):
        steps = jax.random.uniform(jax.random.fold_in(jax.random.fold_in(own_key, 6), axis_at), (shards_of,), jnp.float32, least / len(cuts), high / len(cuts))
        return jnp.repeat(jnp.exp(steps), extent[axis_at] // shards_of).reshape((-1,) + (1,) * (len(extent) - axis_at - 1))

    level = one(*cuts[0])
    for cut in cuts[1:]:
        level = level * one(*cut)
    return level


def length_profile(amount, total, reach, lean):
    portions = [(1 << 20) // math.isqrt(grade ** lean) + 1 for grade in range(2, amount + 1)]
    rest, holding = total - reach - (amount - 1), [1] * (amount - 1)
    while rest > 0:
        movable = [i for i in range(amount - 1) if holding[i] < reach]
        mass, remaining = sum([portions[i] for i in movable]), rest
        for i in movable:
            addition = min(reach - holding[i], max(1, remaining * portions[i] // mass), rest)
            holding[i] = holding[i] + addition
            rest = rest - addition
    return np.array([reach] + holding)


def uneven_parts(own_key, amount, total, reach, skew):
    if amount == 2:
        one = jax.random.randint(own_key, (), max(1, total - reach), min(reach, total - 1) + 1)
        return jnp.stack([one, total - one])
    lengths = jnp.asarray(length_profile(amount, total, reach, skew), jnp.int32)
    pairs = (amount - 1) // 2
    donor, receiver = lengths[1:1 + 2 * pairs:2], lengths[2:2 + 2 * pairs:2]
    slack = jnp.minimum(donor - 1, reach - receiver)
    shifted = jax.random.randint(jax.random.fold_in(own_key, 1), (pairs,), 0, 1 << 20) % (slack + 1)
    lengths = lengths.at[1:1 + 2 * pairs:2].set(donor - shifted).at[2:2 + 2 * pairs:2].set(receiver + shifted)
    return lengths[jax.random.permutation(jax.random.fold_in(own_key, 2), amount)]


def scatter_about(own_key, shape, deviation, reach, shards=(), dtype=jnp.bfloat16):
    entries = deviation * jax.random.normal(own_key, shape, jnp.float32)
    if shards:
        entries = entries * shard_levels(own_key, shape, shards, -0.22, 0.18)
    return jnp.clip(entries, -reach, reach).astype(dtype)


def setup_inputs(seed: int = 0) -> dict:
    key_of = jax.random.split(jax.random.key(seed), 19)
    tokens = scatter_about(key_of[0], (SEQS, LEN, D), 1.0, 6.0, ((0, 8), (1, 4)))
    segment_ids = jax.vmap(lambda own: jnp.searchsorted(jnp.cumsum(uneven_parts(own, DOCS, LEN, LEN // 2, 0)), jnp.arange(LEN), side="right"))(jax.random.split(key_of[1], SEQS)).reshape((SEQS, LEN)).astype(jnp.int32)
    query_weight = scatter_about(key_of[2], (D, D), (D // 4) ** -0.5, 0.4375, ((0, 8),))
    key_weight = scatter_about(key_of[3], (D, D), D ** -0.5, 0.21875, ((0, 8),))
    value_weight = scatter_about(key_of[4], (D, D), D ** -0.5, 0.21875, ((0, 8),))
    merge_weight = scatter_about(key_of[5], (D, D), (D // 16) ** -0.5, 0.875, ((0, 8),))
    query_bias = scatter_about(key_of[6], (D,), 0.5, 3.0, ((0, 8),))
    value_bias = scatter_about(key_of[7], (D,), 0.5, 3.0, ((0, 8),))
    merge_bias = scatter_about(key_of[8], (D,), 0.5, 3.0, ((0, 8),))
    first_gain = jnp.clip(1.0 + 0.1 * jax.random.normal(key_of[9], (D,), jnp.float32), 0.5, 1.5).astype(jnp.bfloat16)
    first_shift = scatter_about(key_of[10], (D,), 0.5, 3.0, ((0, 8),))
    expand_weight = scatter_about(key_of[11], (D, FF), D ** -0.5, 0.21875, ((0, 8),))
    expand_bias = scatter_about(key_of[12], (FF,), 0.5, 3.0, ((0, 8),))
    shrink_weight = scatter_about(key_of[13], (FF, D), (FF // 4) ** -0.5, 0.21875, ((0, 8),))
    shrink_bias = scatter_about(key_of[14], (D,), 0.5, 3.0, ((0, 8),))
    second_gain = jnp.clip(1.0 + 0.1 * jax.random.normal(key_of[15], (D,), jnp.float32), 0.5, 1.5).astype(jnp.bfloat16)
    second_shift = scatter_about(key_of[16], (D,), 0.5, 3.0, ((0, 8),))
    cotangent = scatter_about(key_of[17], (SEQS, LEN, D), 1.0, 6.0, ((0, 8), (1, 4)))
    return dict(tokens=tokens, segment_ids=segment_ids, query_weight=query_weight, key_weight=key_weight, value_weight=value_weight, merge_weight=merge_weight, query_bias=query_bias, value_bias=value_bias, merge_bias=merge_bias, first_gain=first_gain, first_shift=first_shift, expand_weight=expand_weight, expand_bias=expand_bias, shrink_weight=shrink_weight, shrink_bias=shrink_bias, second_gain=second_gain, second_shift=second_shift, cotangent=cotangent)


@jax.custom_vjp
def low(v):
    return lax.optimization_barrier(v.astype(jnp.bfloat16)).astype(jnp.float32)

@jax.custom_vjp
def low_back(v):
    return v

def low_keep(v):
    return (low(v), None)

def low_pass(kept, grad):
    return (grad,)

def back_keep(v):
    return (v, None)

def back_low(kept, grad):
    return (low(grad),)
low.defvjp(low_keep, low_pass)
low_back.defvjp(back_keep, back_low)

def matmul(left, right):
    return jnp.dot(left, right, precision=lax.Precision.HIGHEST)

def layer_norm(values, gain, shift):
    center = values - lax.optimization_barrier(jnp.mean(values, axis=-1, keepdims=True))
    spread = lax.optimization_barrier(jnp.mean(center * center, axis=-1, keepdims=True))
    return center * lax.rsqrt(spread + 1e-12) * gain + shift

def attend(query, key, value, segs):
    block = min(512, LEN)
    count = LEN // block
    q_blocks = query.reshape(count, block, HEADS, HEAD_DIM)
    s_blocks = segs.reshape(count, block)
    keys = key.reshape(LEN, HEADS, HEAD_DIM)
    values = value.reshape(LEN, HEADS, HEAD_DIM)

    def one_block(item):
        q_block, s_block = item
        raw = jnp.einsum('qhd,khd->hqk', q_block, keys, precision=lax.Precision.HIGHEST)
        scores = low_back(raw * 0.125)
        same = (s_block[:, None] == segs[None, :])[None]
        scores = jnp.where(same, scores, -1000000000.0)
        top = lax.optimization_barrier(jnp.max(scores, axis=-1, keepdims=True))
        expo = jnp.exp(scores - top)
        prob = expo / lax.optimization_barrier(jnp.sum(expo, axis=-1, keepdims=True))
        return jnp.einsum('hqk,khd->qhd', low(prob), values, precision=lax.Precision.HIGHEST)
    mixed = lax.map(jax.checkpoint(one_block), (q_blocks, s_blocks))
    return mixed.reshape(LEN, HEADS * HEAD_DIM)

def forward(inputs, segs, params):
    wq, wk, wv, wo, bq, bv, bo, g_one, s_one, w_in, b_in, w_out, b_out, g_two, s_two = params
    query = low_back(low(matmul(inputs, wq) + bq))
    key = low_back(low(matmul(inputs, wk)))
    value = low_back(low(matmul(inputs, wv) + bv))
    attended = low_back(low(attend(query, key, value, segs)))
    branch = low_back(matmul(attended, wo) + bo)
    first = layer_norm(inputs + branch, g_one, s_one)
    pre = low_back(matmul(low(first), w_in) + b_in)
    act = low(jax.nn.gelu(pre, approximate=False))
    shrunk = low_back(matmul(act, w_out) + b_out)
    return layer_norm(first + shrunk, g_two, s_two)

def reference(tokens, segment_ids, query_weight, key_weight, value_weight, merge_weight, query_bias, value_bias, merge_bias, first_gain, first_shift, expand_weight, expand_bias, shrink_weight, shrink_bias, second_gain, second_shift, cotangent):
    params = tuple((p.astype(jnp.float32) for p in (query_weight, key_weight, value_weight, merge_weight, query_bias, value_bias, merge_bias, first_gain, first_shift, expand_weight, expand_bias, shrink_weight, shrink_bias, second_gain, second_shift)))

    def one_seq(carry, item):
        inputs, segs, grad_out = item

        def run(values, weights):
            return forward(values, segs, weights)
        result, pull = jax.vjp(run, inputs.astype(jnp.float32), params)
        d_input, d_params = pull(grad_out.astype(jnp.float32))
        carry = jax.tree.map(jnp.add, carry, d_params)
        return (carry, (result.astype(jnp.bfloat16), d_input.astype(jnp.bfloat16)))
    zeros = tuple((jnp.zeros(p.shape, jnp.float32) for p in params))
    grads, (outputs, input_grads) = lax.scan(one_seq, zeros, (tokens, segment_ids, cotangent))
    return (outputs, input_grads, grads[0], grads[1], grads[2], grads[3], grads[4], grads[5], grads[6], grads[7], grads[8], grads[9], grads[10], grads[11], grads[12], grads[13], grads[14])
```

```python
from functools import partial

import jax
import jax.numpy as jnp
from jax import lax
from jax.experimental import pallas as pl
from jax.experimental.pallas import tpu as pltpu
from jax.sharding import PartitionSpec as P

HEAD_DIM = 64
LOW = jnp.bfloat16
FULL = jnp.float32
VMEM = pl.BlockSpec(memory_space=pltpu.VMEM)
SMEM = pl.BlockSpec(memory_space=pltpu.SMEM)
CORE_PAIRS = [(0, 1), (1, 0), (2, 3), (3, 2)]
CHIP_PAIRS = [(0, 2), (2, 0), (1, 3), (3, 1)]
EXTRA = 8
FAR = -1e9


def nn(a, b):
    return lax.dot_general(a, b, (((1,), (0,)), ((), ())), preferred_element_type=FULL)


def nt(a, b):
    return lax.dot_general(a, b, (((1,), (1,)), ((), ())), preferred_element_type=FULL)


def tn(a, b):
    return lax.dot_general(a, b, (((0,), (0,)), ((), ())), preferred_element_type=FULL)


def rows_at(block, size):
    return pl.ds(pl.multiple_of(block * size, size), size)


def call(kernel, name, outs, table, *args, scratch=(), flops=0, nbytes=0):
    return pl.pallas_call(
        kernel,
        name=name,
        out_shape=[jax.ShapeDtypeStruct(shape, dtype) for shape, dtype in outs],
        in_specs=[SMEM] + [VMEM] * len(args),
        out_specs=[VMEM] * len(outs),
        scratch_shapes=[pltpu.VMEM(shape, dtype) for shape, dtype in scratch],
        cost_estimate=pl.CostEstimate(
            flops=int(flops), bytes_accessed=int(nbytes), transcendentals=0
        ),
    )(table, *args)


def attend_kernel(parts, table, t0, t1, t2, t3, *refs):
    pieces, refs = refs[:parts], refs[parts:]
    tok, w, qp, kp, v, q_t, k_t, o_t, lse, keep, send, heads, v_t = refs
    seq, y = table[0], table[1]
    rows = t0.shape[0]
    width = w.shape[0]
    piece = width // parts
    length = tok.shape[0]
    for j, t in enumerate((t0, t1, t2, t3)):
        tok[rows_at(seq ^ j, rows), :] = t[...]
    bias = jnp.zeros((EXTRA, w.shape[1]), FULL)
    for p, ref in enumerate(pieces):
        w[rows_at(table[4 + p], piece), :] = ref[:piece, :]
        bias = bias + ref[piece : piece + EXTRA, :].astype(FULL)
    bias = bias[0:1, :]
    lane = lax.broadcasted_iota(jnp.int32, (rows, 256), 1)
    mark = (lane - 192).astype(FULL)
    for i in range(length // rows):
        here = slice(i * rows, (i + 1) * rows)
        x = nn(tok[here, :width], w[...]) + bias
        seg = tok[here, width : width + 128].astype(FULL)
        seg = jnp.concatenate([seg, seg], axis=1)
        q = x[:, :256].astype(LOW).astype(FULL) * 0.125
        q = jnp.where(lane < 192, q, jnp.where((lane < 196) & (mark != seg), FAR, 0.0))
        k = pltpu.roll(x[:, 128:384], 192, 1).astype(LOW).astype(FULL)
        k = jnp.where(lane < 192, k, jnp.where(mark == seg, 1.0, 0.0))
        vv = x[:, 384:640]
        qp[here, :] = q.astype(LOW)
        kp[here, :] = k.astype(LOW)
        v[here, :] = vv.astype(LOW)
        q_t[:, here] = q.T.astype(LOW)
        k_t[:, here] = k.T.astype(LOW)
        v_t[:, here] = vv.T.astype(LOW)
        for h in range(3):
            heads[h, here, :] = jnp.where(
                (lane // HEAD_DIM == h) | (lane >= 192), k, 0.0
            ).astype(LOW)
    lse[...] = jnp.zeros(lse.shape, FULL)

    @pl.loop(0, length // 256)
    def _(i):
        cols = rows_at(i, 256)
        for h in range(3):
            mine = slice(HEAD_DIM * h, HEAD_DIM * (h + 1))
            scores = nn(heads[h], q_t[:, cols])
            top = jnp.max(scores, axis=0, keepdims=True)
            expo = jnp.exp(scores - top)
            total = jnp.sum(expo, axis=0, keepdims=True)
            mixed = nn(v_t[mine, :], expo.astype(LOW))
            o_t[mine, cols] = mixed * (1.0 / total)
            lse[h : h + 1, cols] = top + jnp.log(total)

    half = length // 2
    keep[...] = o_t[:, rows_at(y, half)].astype(LOW)
    send[...] = o_t[:, rows_at(1 - y, half)].astype(LOW)


def gelu_parts(u):
    a = jnp.abs(u) * 0.7071067811865476
    t = 1.0 / (1.0 + 0.3275911 * a)
    poly = t * (
        0.254829592
        + t * (-0.284496736 + t * (1.421413741 + t * (-1.453152027 + t * 1.061405429)))
    )
    bell = jnp.exp(-0.5 * u * u)
    tail = 0.5 * poly * bell
    phi = jnp.where(u >= 0, 1.0 - tail, tail)
    return u * phi, phi + u * (bell * 0.3989422804014327)


def expand_kernel(parts, table, a0, a1, a2, a3, tok, other, *refs):
    em, refs = refs[:parts], refs[parts:]
    sh_in, refs = refs[:parts], refs[parts:]
    att, wm, e, sh, vec, normed, rstd, low, act, slope, part = refs
    seq, y, c = table[0], table[1], table[2]
    width = e.shape[0]
    piece = width // parts
    hidden = sh.shape[0]
    hidden_piece = hidden // parts
    half = width // 2
    for j, a in enumerate((a0, a1, a2, a3)):
        att[rows_at(seq ^ j, 192), :] = a[...]
    total = jnp.zeros(vec.shape, FULL)
    for p in range(parts):
        at = rows_at(table[4 + p], piece)
        wm[c, at, :] = em[p][:piece, :half]
        wm[1 - c, at, :] = other[p]
        e[at, :] = em[p][:piece, half:]
        total = total + em[p][piece : piece + EXTRA, :].astype(FULL)
        sh[rows_at(table[4 + p], hidden_piece), :] = sh_in[p][...]
    vec[...] = total
    count = normed.shape[0]
    branch = jnp.concatenate([tn(att[...], wm[0]), tn(att[...], wm[1])], axis=1)
    values = (
        tok[rows_at(y, count), :width].astype(FULL) + branch + vec[0:1, :width]
    )
    center = values - jnp.mean(values, axis=1, keepdims=True)
    scale = lax.rsqrt(jnp.mean(center * center, axis=1, keepdims=True) + 1e-12)
    center = center * scale
    normed[...] = center
    rstd[...] = jnp.broadcast_to(scale, rstd.shape)
    low[...] = (center * vec[1:2, :width] + vec[2:3, :width]).astype(LOW)

    @pl.loop(0, hidden // 256)
    def _(i):
        cols = rows_at(i, 256)
        pre = nn(low[...], e[:, cols]) + vec[6:7, cols]
        value, grad = gelu_parts(pre)
        act[:, cols] = value.astype(LOW)
        slope[:, cols] = grad.astype(LOW)

    part[...] = nn(act[...], sh[...]).astype(LOW)


def second_kernel(table, normed, vec, mine, theirs, cot_mine, cot_theirs, slope, e, sh, *refs):
    out, dsec, dz, dpre, dfp, sums, work = refs
    c = table[2]
    rows = cot_mine.shape[0]
    width = e.shape[0]
    hidden = sh.shape[0]
    first = normed[...] * vec[1:2, :width] + vec[2:3, :width]
    second = first + (mine[...].astype(FULL) + theirs[...].astype(FULL)) + vec[3:4, :width]
    center = second - jnp.mean(second, axis=1, keepdims=True)
    scale = lax.rsqrt(jnp.mean(center * center, axis=1, keepdims=True) + 1e-12)
    center = center * scale
    gain = vec[4:5, :width]
    work[...] = center * gain + vec[5:6, :width]
    out[...] = work[rows_at(c, rows), :].astype(LOW)
    work[rows_at(c, rows), :] = cot_mine[...].astype(FULL)
    work[rows_at(1 - c, rows), :] = cot_theirs[...].astype(FULL)
    up = work[...]
    sums[...] = jnp.zeros(sums.shape, FULL)
    sums[0:1, :width] = jnp.sum(up * center, axis=0, keepdims=True)
    sums[1:2, :width] = jnp.sum(up, axis=0, keepdims=True)
    scaled = up * gain
    grad = scale * (
        scaled
        - jnp.mean(scaled, axis=1, keepdims=True)
        - center * jnp.mean(scaled * center, axis=1, keepdims=True)
    )
    dsec[...] = grad
    dz[...] = grad.astype(LOW)
    sums[2:3, :width] = jnp.sum(dz[...].astype(FULL), axis=0, keepdims=True)

    @pl.loop(0, hidden // 256)
    def _(i):
        cols = rows_at(i, 256)
        value = nt(dz[...], sh[cols, :]) * slope[:, cols].astype(FULL)
        value = value.astype(LOW)
        dpre[:, cols] = value
        sums[3:4, cols] = jnp.sum(value.astype(FULL), axis=0, keepdims=True)

    dfp[...] = nt(dpre[...], e[...]).astype(LOW)


def shrink_grad_kernel(parts, table, act, dz, send, keep, work):
    block = work.shape[0] // parts
    work[...] = tn(act[...], dz[...]).astype(LOW)
    for b in range(parts // 2):
        send[b] = work[rows_at(table[4 + parts + b], block), :]
        keep[b] = work[rows_at(table[4 + parts + parts // 2 + b], block), :]


def first_kernel(table, mine, theirs, dsec, normed, rstd, vec, wm, dres, dbr, dkeep, dsend, sums, work):
    seq, c = table[0], table[2]
    width = normed.shape[1]
    half = width // 2
    rows = dres.shape[0]
    up = (mine[...].astype(FULL) + theirs[...].astype(FULL)) + dsec[...]
    center = normed[...]
    sums[...] = jnp.zeros(sums.shape, FULL)
    sums[0:1, :] = jnp.sum(up * center, axis=0, keepdims=True)
    sums[1:2, :] = jnp.sum(up, axis=0, keepdims=True)
    scaled = up * vec[1:2, :width]
    work[...] = rstd[:, 0:1] * (
        scaled
        - jnp.mean(scaled, axis=1, keepdims=True)
        - center * jnp.mean(scaled * center, axis=1, keepdims=True)
    )
    dbr[...] = work[...].astype(LOW)
    dres[...] = work[rows_at(c, rows), :]
    sums[2:3, :] = jnp.sum(dbr[...].astype(FULL), axis=0, keepdims=True)
    for j, ref in ((0, dkeep), (2, dsend)):
        at = rows_at(seq ^ j, 192)
        ref[...] = (
            nt(wm[0, at, :], dbr[:, :half]) + nt(wm[1, at, :], dbr[:, half:])
        ).astype(LOW)


def expand_grad_kernel(parts, table, low, dpre, att, dbr, sums_two, sums_one, send, keep, work, rows):
    c = table[2]
    width = low.shape[1]
    half = width // 2
    block = width // parts
    work[:, :half] = nn(att[...], dbr[:, rows_at(c, half)]).astype(LOW)
    work[:, half:] = tn(low[...], dpre[...]).astype(LOW)
    rows[...] = jnp.zeros(rows.shape, FULL)
    rows[0:1, :width] = sums_one[2:3, :]
    rows[1:3, :width] = sums_one[0:2, :]
    rows[3:4, :width] = sums_two[2:3, :width]
    rows[4:6, :width] = sums_two[0:2, :width]
    rows[6:7, : dpre.shape[1]] = sums_two[3:4, :]
    for b in range(parts // 2):
        for ref, at in ((send, b), (keep, parts // 2 + b)):
            ref[b, :block, :] = work[rows_at(table[4 + parts + at], block), :]
            ref[b, block:, :] = rows[...].astype(LOW)


def attend_back_kernel(
    parts, table, tok, qp, kp, v, q_t, k_t, o_t, lse, dkeep, dother, *refs
):
    send, keep, grads, probs, dscores, d_t, d_rows, q_rows, heads, v_heads, dq_t, work = refs
    y = table[1]
    length = tok.shape[0]
    width = work.shape[0]
    block = width // parts
    half = length // 2
    d_t[192:, :] = jnp.zeros((64, length), LOW)
    d_t[:192, rows_at(y, half)] = dkeep[...]
    d_t[:192, rows_at(1 - y, half)] = dother[...]
    lane = lax.broadcasted_iota(jnp.int32, (256, 256), 1)
    for i in range(length // 256):
        here = slice(i * 256, (i + 1) * 256)
        d = d_t[:, here].astype(FULL).T
        k = kp[here, :].astype(FULL)
        q = qp[here, :].astype(FULL)
        vv = v[here, :].astype(FULL)
        for h in range(3):
            own = lane // HEAD_DIM == h
            at = slice(h * length + i * 256, h * length + (i + 1) * 256)
            d_rows[at, :] = jnp.where(own, d, 0.0).astype(LOW)
            q_rows[at, :] = jnp.where(own, q, 0.0).astype(LOW)
            heads[h, here, :] = jnp.where(own | (lane >= 192), k, 0.0).astype(LOW)
            v_heads[h, here, :] = jnp.where(own, vv, 0.0).astype(LOW)
    dq_t[192:, :] = jnp.zeros((64, length), FULL)

    @pl.loop(0, length // 256)
    def _(i):
        cols = rows_at(i, 256)
        for h in range(3):
            mine = slice(HEAD_DIM * h, HEAD_DIM * (h + 1))
            out = pl.ds(pl.multiple_of(h * length + i * 256, 256), 256)
            prob = jnp.exp(nn(heads[h], q_t[:, cols]) - lse[h : h + 1, cols])
            probs[:, out] = prob.astype(LOW)
            delta = jnp.sum(
                d_t[mine, cols].astype(FULL) * o_t[mine, cols], axis=0, keepdims=True
            )
            grad = (prob * (nn(v_heads[h], d_t[:, cols]) - delta)).astype(LOW)
            dscores[:, out] = grad
            dq_t[mine, cols] = nn(k_t[mine, :], grad) * 0.125

    for i in range(length // 256):
        here = slice(i * 256, (i + 1) * 256)
        dv = nn(probs[here, :], d_rows[...])
        dk = pltpu.roll(nn(dscores[here, :], q_rows[...]), 192, 1)
        dq = dq_t[:, here].T
        grads[here, :256] = jnp.where(lane < 192, dq, dk).astype(LOW)
        grads[here, 256:384] = dk[:, :128].astype(LOW)
        grads[here, 384:] = dv.astype(LOW)
    work[...] = tn(tok[:, :width], grads[...]).astype(LOW)
    total = jnp.sum(grads[...].astype(FULL), axis=0, keepdims=True)
    total = jnp.broadcast_to(total, (EXTRA, total.shape[1])).astype(LOW)
    for b in range(parts // 2):
        for ref, at in ((send, b), (keep, parts // 2 + b)):
            ref[b, :block, :] = work[rows_at(table[4 + parts + at], block), :]
            ref[b, block:, :] = total


def input_grad_kernel(table, grads, w, send, keep, work):
    seq = table[0]
    rows = send.shape[1]
    work[...] = nt(grads[...], w[...]).astype(LOW)
    for b in range(2):
        send[b] = work[rows_at(seq ^ (1 + 2 * b), rows), :]
        keep[b] = work[rows_at(seq ^ (2 * b), rows), :]


def pair_kernel(table, keep, got, *outs):
    z = table[3]
    ring = keep.shape[0]
    for k, ref in enumerate(outs):
        at = lax.rem(z + k, ring)
        ref[...] = (keep[at].astype(FULL) + got[at].astype(FULL)).astype(LOW)


def swap_core(x):
    return lax.ppermute(x, "seq", CORE_PAIRS)


def swap_chip(x):
    return lax.ppermute(x, "seq", CHIP_PAIRS)


def swap_near(x):
    return lax.ppermute(x, "fsdp", [(i, i ^ 1) for i in range(8)])


def shift(x, k):
    return lax.ppermute(x, "fsdp", [(i, (i + 2 * k) % 8) for i in range(8)])


def gather(shard, count, extra):
    if count == 8:
        mine = [shard] + [shift(shard, k) for k in (1, 2, 3)]
        return mine + [swap_near(m) for m in mine]
    whole = lax.all_gather(shard, "fsdp", axis=0)
    rows = shard.shape[0] - extra
    main = whole[:, :rows].reshape(count * rows, shard.shape[1])
    if not extra:
        return [main]
    rest = jnp.sum(whole[:, rows:].astype(FULL), axis=0).astype(LOW)
    return [jnp.concatenate([main, rest], axis=0)]


def scatter(send, keep, table, count, extra):
    if count == 8:
        got = swap_near(send)
        shape = keep.shape[1:]
        parts = call(pair_kernel, "pair", [(shape, LOW)] * 4, table, keep, got)
        total = parts[0].astype(FULL)
        for k in (1, 2, 3):
            total = total + shift(parts[k], k).astype(FULL)
        return total
    both = jnp.concatenate([send, keep], axis=0)
    rows = both.shape[1] - extra
    main = both[:, :rows].reshape(count, -1, both.shape[2])
    rest = jnp.broadcast_to(both[:1, rows:], (count, extra, both.shape[2]))
    both = jnp.concatenate([main, rest], axis=1)
    return lax.psum_scatter(both, "fsdp", scatter_dimension=0).astype(FULL)


def body(
    count,
    tokens,
    segment_ids,
    query_weight,
    key_weight,
    value_weight,
    merge_weight,
    query_bias,
    value_bias,
    merge_bias,
    first_gain,
    first_shift,
    expand_weight,
    expand_bias,
    shrink_weight,
    shrink_bias,
    second_gain,
    second_shift,
    cotangent,
):
    rows, width = tokens.shape[1:]
    hidden = expand_weight.shape[1]
    share = width // count
    unit = hidden // count // 2
    slim = width // 4
    half = width // 2
    length = 4 * rows
    near = 2 * rows
    seq = lax.axis_index("seq")
    own = lax.axis_index("fsdp")
    c, y = seq % 2, seq // 2
    z, x = own // 2, own % 2
    if count == 8:
        parts, pad, rest = 8, EXTRA, 0
        mine = [((z - k) % 4) * 2 + x for k in range(4)]
        pieces = mine + [2 * (m // 2) + 1 - x for m in mine]
        blocks = [2 * k + 1 - x for k in range(4)] + [2 * k + x for k in range(4)]
    else:
        parts, pad = 2, EXTRA
        pieces, blocks = [0, 0], [0, 1]
    table = jnp.stack([seq, y, c, z] + pieces + blocks).astype(jnp.int32)
    pieces_in = parts if count == 8 else 1
    if count != 8:
        table_in = jnp.stack([seq, y, c, z, 0]).astype(jnp.int32)
    else:
        table_in = table

    def columns(weight):
        return lax.dynamic_slice(weight, (0, slim * seq), (share, slim))

    pair = jnp.stack([query_bias, value_bias])
    pair = lax.dynamic_update_slice(jnp.zeros((2, width), LOW), pair, (0, share * own))
    pair = lax.dynamic_slice(pair, (0, slim * seq), (2, slim))
    blank = jnp.zeros((1, slim), LOW)
    bias_row = jnp.concatenate(
        [pair[0:1], blank, pair[1:2], jnp.zeros((1, 64), LOW)], axis=1
    )
    shard = jnp.concatenate(
        [
            columns(query_weight),
            columns(key_weight),
            columns(value_weight),
            jnp.zeros((share, 64), LOW),
        ],
        axis=1,
    )
    shard = jnp.concatenate([shard, jnp.pad(bias_row, ((0, EXTRA - 1), (0, 0)))], axis=0)
    w_pieces = gather(shard, count, EXTRA)

    inputs = tokens.reshape(rows, width)
    marks = jnp.broadcast_to(segment_ids.reshape(rows, 1).astype(LOW), (rows, 128))
    inputs = jnp.concatenate([inputs, marks], axis=1)
    t_two = swap_chip(inputs)
    t_one = swap_core(inputs)
    t_three = swap_core(t_two)

    vectors = jnp.zeros((EXTRA, half + hidden // 2), LOW)
    stack = jnp.stack(
        [merge_bias, first_gain, first_shift, shrink_bias, second_gain, second_shift]
    )
    vectors = lax.dynamic_update_slice(vectors, stack, (0, share * own))
    chunk = lax.dynamic_slice(expand_bias, (unit * c,), (unit,)).reshape(1, unit)
    vectors = lax.dynamic_update_slice(vectors, chunk, (6, unit * own))
    wide = expand_weight.reshape(share, count, 2, unit)
    wide = jnp.where(c == 0, wide[:, :, 0], wide[:, :, 1]).reshape(share, hidden // 2)
    em = jnp.concatenate(
        [lax.dynamic_slice(merge_weight, (0, half * c), (share, half)), wide], axis=1
    )
    em = jnp.concatenate([em, vectors], axis=0)
    em_pieces = gather(em, count, EXTRA)
    low_shard = lax.dynamic_slice(shrink_weight, (unit * c, 0), (unit, width))
    sh_pieces = gather(low_shard, count, 0)

    tok, w, qp, kp, v, q_t, k_t, o_t, lse, keep, send = call(
        partial(attend_kernel, pieces_in),
        "attend",
        [
            ((length, width + 128), LOW),
            ((width, 640), LOW),
            ((length, 256), LOW),
            ((length, 256), LOW),
            ((length, 256), LOW),
            ((256, length), LOW),
            ((256, length), LOW),
            ((slim, length), FULL),
            ((8, length), FULL),
            ((slim, near), LOW),
            ((slim, near), LOW),
        ],
        table_in,
        inputs,
        t_one,
        t_two,
        t_three,
        *w_pieces,
        scratch=[((3, length, 256), LOW), ((256, length), LOW)],
        flops=4e9,
        nbytes=1e7,
    )
    a_two = swap_chip(send)
    a_one = swap_core(keep)
    a_three = swap_core(a_two)
    merge_other = swap_core(jnp.stack([p[: width // pieces_in, :half] for p in em_pieces]))
    cot = cotangent.reshape(rows, width)
    cot_other = swap_core(cot)

    att, wm, e, sh, vec, normed, rstd, low, act, slope, part = call(
        partial(expand_kernel, pieces_in),
        "expand",
        [
            ((width, near), LOW),
            ((2, width, half), LOW),
            ((width, hidden // 2), LOW),
            ((hidden // 2, width), LOW),
            ((EXTRA, half + hidden // 2), FULL),
            ((near, width), FULL),
            ((near, 128), FULL),
            ((near, width), LOW),
            ((near, hidden // 2), LOW),
            ((near, hidden // 2), LOW),
            ((near, width), LOW),
        ],
        table_in,
        keep,
        a_one,
        a_two,
        a_three,
        tok,
        merge_other,
        *em_pieces,
        *sh_pieces,
        flops=4e9,
        nbytes=2e7,
    )
    part_other = swap_core(part)
    out, dsec, dz, dpre, dfp, sums_two = call(
        second_kernel,
        "second",
        [
            ((rows, width), LOW),
            ((near, width), FULL),
            ((near, width), LOW),
            ((near, hidden // 2), LOW),
            ((near, width), LOW),
            ((EXTRA, hidden // 2), FULL),
        ],
        table,
        normed,
        vec,
        part,
        part_other,
        cot,
        cot_other,
        slope,
        e,
        sh,
        scratch=[((near, width), FULL)],
        flops=3e9,
        nbytes=2e7,
    )
    dfp_other = swap_core(dfp)
    sh_send, sh_keep = call(
        partial(shrink_grad_kernel, parts),
        "shrink_grad",
        [((parts // 2, hidden // 2 // parts, width), LOW)] * 2,
        table,
        act,
        dz,
        scratch=[((hidden // 2, width), LOW)],
        flops=1.2e9,
        nbytes=5e6,
    )
    dres, dbr, dkeep, dsend, sums_one = call(
        first_kernel,
        "first",
        [
            ((rows, width), FULL),
            ((near, width), LOW),
            ((slim, near), LOW),
            ((slim, near), LOW),
            ((EXTRA, width), FULL),
        ],
        table,
        dfp,
        dfp_other,
        dsec,
        normed,
        rstd,
        vec,
        wm,
        scratch=[((near, width), FULL)],
        flops=1e9,
        nbytes=8e6,
    )
    dother = swap_chip(dsend)
    shrink_own = scatter(sh_send, sh_keep, table, count, 0)
    em_send, em_keep = call(
        partial(expand_grad_kernel, parts),
        "expand_grad",
        [((parts // 2, width // parts + EXTRA, half + hidden // 2), LOW)] * 2,
        table,
        low,
        dpre,
        att,
        dbr,
        sums_two,
        sums_one,
        scratch=[((width, half + hidden // 2), LOW), ((EXTRA, half + hidden // 2), FULL)],
        flops=1.5e9,
        nbytes=8e6,
    )
    em_own = scatter(em_send, em_keep, table, count, EXTRA)
    w_send, w_keep, grads = call(
        partial(attend_back_kernel, parts),
        "attend_back",
        [((parts // 2, width // parts + EXTRA, 640), LOW)] * 2 + [((length, 640), LOW)],
        table,
        tok,
        qp,
        kp,
        v,
        q_t,
        k_t,
        o_t,
        lse,
        dkeep,
        dother,
        scratch=[
            ((length, 3 * length), LOW),
            ((length, 3 * length), LOW),
            ((256, length), LOW),
            ((3 * length, 256), LOW),
            ((3 * length, 256), LOW),
            ((3, length, 256), LOW),
            ((3, length, 256), LOW),
            ((256, length), FULL),
            ((width, 640), LOW),
        ],
        flops=8e9,
        nbytes=1e7,
    )
    w_own = scatter(w_send, w_keep, table, count, EXTRA).astype(LOW)
    x_send, x_keep = call(
        input_grad_kernel,
        "input_grad",
        [((2, rows, width), LOW)] * 2,
        table,
        grads,
        w,
        scratch=[((length, width), LOW)],
        flops=1e9,
        nbytes=5e6,
    )
    x_sum = x_keep.astype(FULL) + swap_core(x_send).astype(FULL)
    x_other = swap_chip(x_sum[1].astype(LOW))
    in_grad = dres + x_sum[0] + x_other.astype(FULL)

    def over_chips(part):
        part = part.astype(LOW)
        return part.astype(FULL) + swap_chip(part).astype(FULL)

    def both_cores(part):
        other = swap_core(part)
        return jnp.where(c == 0, part, other), jnp.where(c == 0, other, part)

    sh_low, sh_high = both_cores(over_chips(shrink_own))
    d_shrink = jnp.concatenate([sh_low, sh_high], axis=0)
    em_low, em_high = both_cores(over_chips(em_own))
    d_merge = jnp.concatenate([em_low[:share, :half], em_high[:share, :half]], axis=1)
    d_expand = jnp.stack(
        [
            em_low[:share, half:].reshape(share, count, unit),
            em_high[:share, half:].reshape(share, count, unit),
        ],
        axis=2,
    ).reshape(share, hidden)
    small = lax.dynamic_slice(em_low[share:], (0, share * own), (6, share))
    d_b_expand = jnp.concatenate(
        [
            lax.dynamic_slice(part[share:], (6, unit * own), (1, unit)).reshape(unit)
            for part in (em_low, em_high)
        ]
    )

    w_two = swap_chip(w_own)
    w_one = swap_core(w_own)
    w_three = swap_core(w_two)
    near_low = jnp.where(c == 0, w_own, w_one)
    near_high = jnp.where(c == 0, w_one, w_own)
    far_low = jnp.where(c == 0, w_two, w_three)
    far_high = jnp.where(c == 0, w_three, w_two)
    ordered = [
        jnp.where(y == 0, near_low, far_low),
        jnp.where(y == 0, near_high, far_high),
        jnp.where(y == 0, far_low, near_low),
        jnp.where(y == 0, far_high, near_high),
    ]
    d_q, d_k, d_v = [
        jnp.concatenate([o[:, slim * i : slim * (i + 1)] for o in ordered], axis=1).astype(FULL)
        for i in range(3)
    ]
    d_b_query = lax.dynamic_slice(d_q[share], (share * own,), (share,))
    d_b_value = lax.dynamic_slice(d_v[share], (share * own,), (share,))

    return (
        out.reshape(1, rows, width),
        in_grad.astype(LOW).reshape(1, rows, width),
        d_q[:share],
        d_k[:share],
        d_v[:share],
        d_merge,
        d_b_query,
        d_b_value,
        small[0],
        small[1],
        small[2],
        d_expand,
        d_b_expand,
        d_shrink,
        small[3],
        small[4],
        small[5],
    )


def solution(mesh):
    row, flat = P("fsdp", None), P("fsdp")
    cube = P("fsdp", "seq", None)
    return jax.shard_map(
        partial(body, mesh.shape["fsdp"]),
        mesh=mesh,
        in_specs=(cube, P("fsdp", "seq"))
        + (row,) * 4
        + (flat,) * 5
        + (row, flat, row)
        + (flat,) * 3
        + (cube,),
        out_specs=(cube, cube) + (row,) * 4 + (flat,) * 5 + (row, flat, row) + (flat,) * 3,
        check_vma=False,
    )
```

```python
from functools import partial

import jax
import jax.numpy as jnp
from jax import lax
from jax.experimental import pallas as pl
from jax.experimental.pallas import tpu as pltpu
from jax.sharding import PartitionSpec as P

HEAD_DIM = 64
LOW = jnp.bfloat16
FULL = jnp.float32
VMEM = pl.BlockSpec(memory_space=pltpu.VMEM)
SMEM = pl.BlockSpec(memory_space=pltpu.SMEM)
CORE_PAIRS = [(0, 1), (1, 0), (2, 3), (3, 2)]
CHIP_PAIRS = [(0, 2), (2, 0), (1, 3), (3, 1)]
EXTRA = 8
HEADER = 16
FAR = -1e9


def nn(a, b):
    return lax.dot_general(a, b, (((1,), (0,)), ((), ())), preferred_element_type=FULL)


def nt(a, b):
    return lax.dot_general(a, b, (((1,), (1,)), ((), ())), preferred_element_type=FULL)


def tn(a, b):
    return lax.dot_general(a, b, (((0,), (0,)), ((), ())), preferred_element_type=FULL)


def rows_at(block, size):
    return pl.ds(pl.multiple_of(block * size, size), size)


def call(kernel, name, outs, table, *args, scratch=(), flops=0, nbytes=0):
    return pl.pallas_call(
        kernel,
        name=name,
        out_shape=[jax.ShapeDtypeStruct(shape, dtype) for shape, dtype in outs],
        in_specs=[SMEM] + [VMEM] * len(args),
        out_specs=[VMEM] * len(outs),
        scratch_shapes=[pltpu.VMEM(shape, dtype) for shape, dtype in scratch],
        cost_estimate=pl.CostEstimate(
            flops=0, bytes_accessed=0, transcendentals=0
        ),
    )(table, *args)


def attend_kernel(parts, table, t0, t1, t2, t3, *refs):
    pieces, refs = refs[:parts], refs[parts:]
    tok, w, wm, vec, qp, kp, v, q_t, k_t, o_t, lse, keep, send, heads, v_t = refs
    seq, y = table[0], table[1]
    rows = t0.shape[0]
    width = w.shape[0]
    piece = width // parts
    length = tok.shape[0]
    for j, t in enumerate((t0, t1, t2, t3)):
        tok[rows_at(seq ^ j, rows), :] = t[...]
    total = jnp.zeros(vec.shape, FULL)
    for p, ref in enumerate(pieces):
        at = rows_at(table[4 + p], piece)
        w[at, :] = ref[:piece, :640]
        wm[at, :] = ref[:piece, 640:]
        total = total + ref[piece : piece + HEADER, :].astype(FULL)
    vec[...] = total
    bias = vec[8:9, :640]
    lane = lax.broadcasted_iota(jnp.int32, (rows, 256), 1)
    mark = (lane - 192).astype(FULL)
    for i in range(length // rows):
        here = slice(i * rows, (i + 1) * rows)
        x = nn(tok[here, :width], w[...]) + bias
        seg = tok[here, width : width + 128].astype(FULL)
        seg = jnp.concatenate([seg, seg], axis=1)
        q = x[:, :256].astype(LOW).astype(FULL) * 0.125
        q = jnp.where(lane < 192, q, jnp.where((lane < 196) & (mark != seg), FAR, 0.0))
        k = pltpu.roll(x[:, 128:384], 192, 1).astype(LOW).astype(FULL)
        k = jnp.where(lane < 192, k, jnp.where(mark == seg, 1.0, 0.0))
        vv = x[:, 384:640]
        qp[here, :] = q.astype(LOW)
        kp[here, :] = k.astype(LOW)
        v[here, :] = vv.astype(LOW)
        q_t[:, here] = q.T.astype(LOW)
        k_t[:, here] = k.T.astype(LOW)
        v_t[:, here] = vv.T.astype(LOW)
        for h in range(3):
            heads[h, here, :] = jnp.where(
                (lane // HEAD_DIM == h) | (lane >= 192), k, 0.0
            ).astype(LOW)
    lse[...] = jnp.zeros(lse.shape, FULL)

    @pl.loop(0, length // 256)
    def _(i):
        cols = rows_at(i, 256)
        for h in range(3):
            mine = slice(HEAD_DIM * h, HEAD_DIM * (h + 1))
            scores = nn(heads[h], q_t[:, cols])
            top = jnp.max(scores, axis=0, keepdims=True)
            expo = jnp.exp(scores - top)
            total = jnp.sum(expo, axis=0, keepdims=True)
            mixed = nn(v_t[mine, :], expo.astype(LOW))
            o_t[mine, cols] = mixed * (1.0 / total)
            lse[h : h + 1, cols] = top + jnp.log(total)

    half = length // 2
    keep[...] = o_t[:, rows_at(y, half)].astype(LOW)
    send[...] = o_t[:, rows_at(1 - y, half)].astype(LOW)


def gelu_parts(u):
    phi = 0.5 + 0.5 * lax.erf(u * 0.7071067811865476)
    bell = jnp.exp(-0.5 * u * u)
    return u * phi, phi + u * (bell * 0.3989422804014327)


def merge_kernel(table, a0, a1, a2, a3, tok, vec, mine, theirs, att, normed, rstd, low, bias, work):
    seq, y, c = table[0], table[1], table[2]
    count, width = normed.shape
    half = width // 2
    for j, a in enumerate((a0, a1, a2, a3)):
        att[rows_at(seq ^ j, 192), :] = a[...]
    bias[...] = jnp.broadcast_to(
        jnp.concatenate([vec[6:7, :width], vec[7:8, :width]], axis=1), bias.shape
    )
    work[:, rows_at(c, half)] = tn(att[...], mine[...])
    work[:, rows_at(1 - c, half)] = tn(att[...], theirs[...])
    values = tok[rows_at(y, count), :width].astype(FULL) + work[...] + vec[0:1, :width]
    center = values - jnp.mean(values, axis=1, keepdims=True)
    scale = lax.rsqrt(jnp.mean(center * center, axis=1, keepdims=True) + 1e-12)
    center = center * scale
    normed[...] = center
    rstd[...] = jnp.broadcast_to(scale, rstd.shape)
    low[...] = (center * vec[1:2, :width] + vec[2:3, :width]).astype(LOW)


def gelu_kernel(parts, table, low, bias, *refs):
    pieces, (e, act, slope) = refs[:parts], refs[parts:]
    piece = e.shape[0] // parts
    for p, ref in enumerate(pieces):
        e[rows_at(table[4 + p], piece), :] = ref[...]

    @pl.loop(0, act.shape[1] // 256)
    def _(i):
        cols = rows_at(i, 256)
        pre = nn(low[...], e[:, cols]) + bias[0:1, cols]
        value, grad = gelu_parts(pre)
        act[:, cols] = value.astype(LOW)
        slope[:, cols] = grad.astype(LOW)


def shrink_kernel(parts, table, act, *refs):
    pieces, (sh, part) = refs[:parts], refs[parts:]
    piece = sh.shape[0] // parts
    for p, ref in enumerate(pieces):
        sh[rows_at(table[4 + p], piece), :] = ref[...]
    part[...] = nn(act[...], sh[...]).astype(LOW)


def second_kernel(table, normed, vec, mine, theirs, cot_mine, cot_theirs, *refs):
    out, dsec, dz, sums, work = refs
    c = table[2]
    rows = cot_mine.shape[0]
    width = normed.shape[1]
    first = normed[...] * vec[1:2, :width] + vec[2:3, :width]
    second = first + (mine[...].astype(FULL) + theirs[...].astype(FULL)) + vec[3:4, :width]
    center = second - jnp.mean(second, axis=1, keepdims=True)
    scale = lax.rsqrt(jnp.mean(center * center, axis=1, keepdims=True) + 1e-12)
    center = center * scale
    gain = vec[4:5, :width]
    work[...] = center * gain + vec[5:6, :width]
    out[...] = work[rows_at(c, rows), :].astype(LOW)
    work[rows_at(c, rows), :] = cot_mine[...].astype(FULL)
    work[rows_at(1 - c, rows), :] = cot_theirs[...].astype(FULL)
    up = work[...]
    sums[...] = jnp.zeros(sums.shape, FULL)
    sums[0:1, :] = jnp.sum(up * center, axis=0, keepdims=True)
    sums[1:2, :] = jnp.sum(up, axis=0, keepdims=True)
    scaled = up * gain
    grad = scale * (
        scaled
        - jnp.mean(scaled, axis=1, keepdims=True)
        - center * jnp.mean(scaled * center, axis=1, keepdims=True)
    )
    dsec[...] = grad
    dz[...] = grad.astype(LOW)
    sums[2:3, :] = jnp.sum(dz[...].astype(FULL), axis=0, keepdims=True)


def hidden_kernel(table, dz, slope, e, sh, dpre, dfp, sums):
    hidden = sh.shape[0]
    sums[...] = jnp.zeros(sums.shape, FULL)

    @pl.loop(0, hidden // 256)
    def _(i):
        cols = rows_at(i, 256)
        value = nt(dz[...], sh[cols, :]) * slope[:, cols].astype(FULL)
        value = value.astype(LOW)
        dpre[:, cols] = value
        sums[0:1, cols] = jnp.sum(value.astype(FULL), axis=0, keepdims=True)

    dfp[...] = nt(dpre[...], e[...]).astype(LOW)


def put_blocks(parts, table, work, block, outs, extra=None):
    for i, ref in enumerate(outs):
        for j in range(parts // 4):
            at = table[4 + parts + i * (parts // 4) + j]
            ref[j, :block, :] = work[rows_at(at, block), :]
            if extra is not None:
                ref[j, block:, :] = extra


def shrink_grad_kernel(parts, table, act, dz, *refs):
    outs, work = refs[:4], refs[4]
    work[...] = tn(act[...], dz[...]).astype(LOW)
    put_blocks(parts, table, work, work.shape[0] // parts, outs)


def first_kernel(
    table, mine, theirs, dsec, normed, rstd, vec, wm, wm_other, dres, dbr, dkeep, dsend, sums, work
):
    seq, c = table[0], table[2]
    width = normed.shape[1]
    half = width // 2
    rows = dres.shape[0]
    up = (mine[...].astype(FULL) + theirs[...].astype(FULL)) + dsec[...]
    center = normed[...]
    sums[...] = jnp.zeros(sums.shape, FULL)
    sums[0:1, :] = jnp.sum(up * center, axis=0, keepdims=True)
    sums[1:2, :] = jnp.sum(up, axis=0, keepdims=True)
    scaled = up * vec[1:2, :width]
    work[...] = rstd[:, 0:1] * (
        scaled
        - jnp.mean(scaled, axis=1, keepdims=True)
        - center * jnp.mean(scaled * center, axis=1, keepdims=True)
    )
    dbr[...] = work[...].astype(LOW)
    dres[...] = work[rows_at(c, rows), :]
    sums[2:3, :] = jnp.sum(dbr[...].astype(FULL), axis=0, keepdims=True)
    for j, ref in ((0, dkeep), (2, dsend)):
        at = rows_at(seq ^ j, 192)
        ref[...] = (
            nt(wm[at, :], dbr[:, rows_at(c, half)])
            + nt(wm_other[at, :], dbr[:, rows_at(1 - c, half)])
        ).astype(LOW)


def expand_grad_kernel(parts, table, low, dpre, att, dbr, sums_two, sums_hid, sums_one, *refs):
    outs, (work, rows) = refs[:4], refs[4:]
    c = table[2]
    width = low.shape[1]
    half = width // 2
    work[:, :half] = nn(att[...], dbr[:, rows_at(c, half)]).astype(LOW)
    work[:, half:] = tn(low[...], dpre[...]).astype(LOW)
    rows[...] = jnp.zeros(rows.shape, FULL)
    rows[0:1, :width] = sums_one[2:3, :]
    rows[1:3, :width] = sums_one[0:2, :]
    rows[3:4, :width] = sums_two[2:3, :]
    rows[4:6, :width] = sums_two[0:2, :]
    rows[6:7, : dpre.shape[1]] = sums_hid[0:1, :]
    put_blocks(parts, table, work, width // parts, outs, rows[...].astype(LOW))


def attend_back_kernel(
    parts, table, tok, qp, kp, v, q_t, k_t, o_t, lse, dkeep, dother, *refs
):
    outs, refs = refs[:4], refs[4:]
    grads, probs, dscores, d_t, d_rows, q_rows, heads, v_heads, dq_t, work = refs
    y = table[1]
    length = tok.shape[0]
    width = work.shape[0]
    block = width // parts
    half = length // 2
    d_t[192:, :] = jnp.zeros((64, length), LOW)
    d_t[:192, rows_at(y, half)] = dkeep[...]
    d_t[:192, rows_at(1 - y, half)] = dother[...]
    lane = lax.broadcasted_iota(jnp.int32, (256, 256), 1)
    for i in range(length // 256):
        here = slice(i * 256, (i + 1) * 256)
        d = d_t[:, here].astype(FULL).T
        k = kp[here, :].astype(FULL)
        q = qp[here, :].astype(FULL)
        vv = v[here, :].astype(FULL)
        for h in range(3):
            own = lane // HEAD_DIM == h
            at = slice(h * length + i * 256, h * length + (i + 1) * 256)
            d_rows[at, :] = jnp.where(own, d, 0.0).astype(LOW)
            q_rows[at, :] = jnp.where(own, q, 0.0).astype(LOW)
            heads[h, here, :] = jnp.where(own | (lane >= 192), k, 0.0).astype(LOW)
            v_heads[h, here, :] = jnp.where(own, vv, 0.0).astype(LOW)
    dq_t[192:, :] = jnp.zeros((64, length), FULL)

    @pl.loop(0, length // 256)
    def _(i):
        cols = rows_at(i, 256)
        for h in range(3):
            mine = slice(HEAD_DIM * h, HEAD_DIM * (h + 1))
            out = pl.ds(pl.multiple_of(h * length + i * 256, 256), 256)
            prob = jnp.exp(nn(heads[h], q_t[:, cols]) - lse[h : h + 1, cols])
            probs[:, out] = prob.astype(LOW)
            delta = jnp.sum(
                d_t[mine, cols].astype(FULL) * o_t[mine, cols], axis=0, keepdims=True
            )
            grad = (prob * (nn(v_heads[h], d_t[:, cols]) - delta)).astype(LOW)
            dscores[:, out] = grad
            dq_t[mine, cols] = nn(k_t[mine, :], grad) * 0.125

    for i in range(length // 256):
        here = slice(i * 256, (i + 1) * 256)
        dv = nn(probs[here, :], d_rows[...])
        dk = pltpu.roll(nn(dscores[here, :], q_rows[...]), 192, 1)
        dq = dq_t[:, here].T
        grads[here, :256] = jnp.where(lane < 192, dq, dk).astype(LOW)
        grads[here, 256:384] = dk[:, :128].astype(LOW)
        grads[here, 384:] = dv.astype(LOW)
    work[...] = tn(tok[:, :width], grads[...]).astype(LOW)
    total = jnp.sum(grads[...].astype(FULL), axis=0, keepdims=True)
    total = jnp.broadcast_to(total, (EXTRA, total.shape[1])).astype(LOW)
    put_blocks(parts, table, work, block, outs, total)


def input_grad_kernel(table, grads, w, send, keep, work):
    seq = table[0]
    rows = send.shape[1]
    work[...] = nt(grads[...], w[...]).astype(LOW)
    for b in range(2):
        send[b] = work[rows_at(seq ^ (1 + 2 * b), rows), :]
        keep[b] = work[rows_at(seq ^ (2 * b), rows), :]


def pair_kernel(keep, got, *outs):
    for k, ref in enumerate(outs):
        ref[...] = (keep[k].astype(FULL) + got[k].astype(FULL)).astype(LOW)


def projection_kernel(table, wq, wk, wv, merge, rest, out):
    seq, c = table[0], table[2]
    share, width = wq.shape
    slim, half = width // 4, width // 2
    for s in range(4):

        @pl.when(seq == s)
        def _():
            cols = slice(slim * s, slim * (s + 1))
            for i, ref in enumerate((wq, wk, wv)):
                out[:share, slim * i : slim * (i + 1)] = ref[:, cols]

    out[:share, 3 * slim : 640] = jnp.zeros((share, 640 - 3 * slim), LOW)
    out[:share, 640:] = merge[:, rows_at(c, half)]
    out[share:, :] = rest[...]


def wide_kernel(unit, table, wide, out):
    c = table[2]
    for s in range(2):

        @pl.when(c == s)
        def _():
            for f in range(out.shape[1] // unit):
                start = 2 * unit * f + unit * s
                out[:, unit * f : unit * (f + 1)] = wide[:, start : start + unit]


def final_projection_kernel(table, p0, p1, p2, p3, dq, dk, dv, rows, stack):
    seq = table[0]
    share = dq.shape[0]
    slim = dq.shape[1] // 4
    for j, p in enumerate((p0, p1, p2, p3)):
        stack[j] = p[...].astype(FULL)
    for i in range(4):
        part = stack[seq ^ i]
        cols = slice(slim * i, slim * (i + 1))
        for g, ref in enumerate((dq, dk, dv)):
            ref[:, cols] = part[:share, slim * g : slim * (g + 1)]
            if g != 1:
                rows[4 * g : 4 * g + 8, cols] = part[share : share + 8, slim * g : slim * (g + 1)]


def final_wide_kernel(table, mine, theirs, merge, wide, rows, both):
    c = table[2]
    share, half = merge.shape[0], merge.shape[1] // 2
    hidden = wide.shape[1]
    unit = hidden // 16
    both[c] = mine[...]
    both[1 - c] = theirs[...]
    for s in range(2):
        merge[:, half * s : half * (s + 1)] = both[s, :share, :half]
        for f in range(8):
            start = half + unit * f
            at = 2 * unit * f + unit * s
            wide[:, at : at + unit] = both[s, :share, start : start + unit]
        rows[s] = both[s, share:, :]


def after(x, *others):
    return lax.optimization_barrier((x,) + others)[0]


class Link:
    def __init__(self, window=2):
        self.window = window
        self.done = []

    def send(self, x, axis, pairs, *others):
        if len(self.done) >= self.window:
            others = others + (self.done[-self.window],)
        if others:
            x = after(x, *others)
        self.done.append(lax.ppermute(x, axis, pairs))
        return self.done[-1]


NEAR_PAIRS = [(i, i ^ 1) for i in range(8)]
SHIFTS = {k: [(i, (i + 2 * k) % 8) for i in range(8)] for k in (1, 2, 3)}


def swap_core(x):
    return lax.ppermute(x, "seq", CORE_PAIRS)


def gather_whole(shard, count, extra):
    whole = lax.all_gather(shard, "fsdp", axis=0)
    rows = shard.shape[0] - extra
    main = whole[:, :rows].reshape(count * rows, shard.shape[1])
    if not extra:
        return [main]
    rest = jnp.sum(whole[:, rows:].astype(FULL), axis=0).astype(LOW)
    return [jnp.concatenate([main, rest], axis=0)]


def scatter_whole(send, keep, count, extra):
    both = jnp.concatenate([send, keep], axis=0)
    rows = both.shape[1] - extra
    main = both[:, :rows].reshape(count, -1, both.shape[2])
    rest = jnp.broadcast_to(both[:1, rows:], (count, extra, both.shape[2]))
    both = jnp.concatenate([main, rest], axis=1)
    return lax.psum_scatter(both, "fsdp", scatter_dimension=0).astype(FULL)


def pair_sum(keep, got):
    shape = keep.shape[1:]
    return pl.pallas_call(
        pair_kernel,
        name="pair",
        out_shape=[jax.ShapeDtypeStruct(shape, LOW)] * keep.shape[0],
        in_specs=[VMEM, VMEM],
        out_specs=[VMEM] * keep.shape[0],
        cost_estimate=pl.CostEstimate(
            flops=0, bytes_accessed=0, transcendentals=0
        ),
    )(keep, got)


def body(
    count,
    tokens,
    segment_ids,
    query_weight,
    key_weight,
    value_weight,
    merge_weight,
    query_bias,
    value_bias,
    merge_bias,
    first_gain,
    first_shift,
    expand_weight,
    expand_bias,
    shrink_weight,
    shrink_bias,
    second_gain,
    second_shift,
    cotangent,
):
    rows, width = tokens.shape[1:]
    hidden = expand_weight.shape[1]
    share = width // count
    unit = hidden // count // 2
    slim = width // 4
    half = width // 2
    length = 4 * rows
    near_rows = 2 * rows
    seq = lax.axis_index("seq")
    own = lax.axis_index("fsdp")
    c, y = seq % 2, seq // 2
    z, x = own // 2, own % 2
    ring = count == 8
    if ring:
        parts = parts_in = 8
        mine = [((z - k) % 4) * 2 + x for k in (0, 1, 3, 2)]
        pieces = mine + [2 * (m // 2) + 1 - x for m in mine]
        there = [2 * ((z + k) % 4) for k in (2, 1, 3, 0)]
        blocks = [t + 1 - x for t in there] + [t + x for t in there]
    else:
        parts, parts_in = 4, 1
        pieces, blocks = [0], [0, 1, 2, 3]
    pieces = pieces + [0] * (parts - parts_in)
    table = jnp.stack([seq, y, c, z] + pieces + blocks).astype(jnp.int32)
    x_link, y_link, z_link = Link(), Link(), Link()

    def near(v, *others):
        return x_link.send(v, "fsdp", NEAR_PAIRS, *others)

    def along(v, k, *others):
        return z_link.send(v, "fsdp", SHIFTS[k], *others)

    def across(v, *others):
        return y_link.send(v, "seq", CHIP_PAIRS, *others)

    pair = jnp.stack([query_bias, value_bias])
    pair = lax.dynamic_update_slice(jnp.zeros((2, width), LOW), pair, (0, share * own))
    pair = lax.dynamic_slice(pair, (0, slim * seq), (2, slim))
    bias_row = jnp.concatenate([pair[0:1], jnp.zeros((1, slim), LOW), pair[1:2]], axis=1)
    rest = jnp.zeros((HEADER, 640 + half), LOW)
    stack = jnp.stack(
        [merge_bias, first_gain, first_shift, shrink_bias, second_gain, second_shift]
    )
    rest = lax.dynamic_update_slice(rest, stack, (0, share * own))
    chunk = lax.dynamic_slice(expand_bias, (unit * c,), (unit,)).reshape(1, unit)
    rest = lax.dynamic_update_slice(
        rest, chunk, (6 + unit * own // width, unit * own % width)
    )
    rest = lax.dynamic_update_slice(rest, bias_row, (8, 0))
    (shard,) = call(
        projection_kernel,
        "projection",
        [((share + HEADER, 640 + half), LOW)],
        table,
        query_weight,
        key_weight,
        value_weight,
        merge_weight,
        rest,
    )
    inputs = tokens.reshape(rows, width)
    marks = jnp.broadcast_to(segment_ids.reshape(rows, 1).astype(LOW), (rows, 128))

    def wide_shard(dep):
        weight = after(expand_weight, dep)
        if ring:
            return call(
                partial(wide_kernel, unit),
                "wide",
                [((share, hidden // 2), LOW)],
                table,
                weight,
            )[0]
        wide = weight.reshape(share, count, 2, unit)
        return jnp.where(c == 0, wide[:, :, 0], wide[:, :, 1]).reshape(share, hidden // 2)

    low_shard = lax.dynamic_slice(shrink_weight, (unit * c, 0), (unit, width))
    if ring:
        q1 = along(shard, 1)
        q3 = along(shard, 3)
        q2 = along(shard, 2)
        qx0 = near(shard)
        inputs = jnp.concatenate([inputs, marks], axis=1)
        t_two = across(inputs)
        t_one = swap_core(inputs)
        qx1 = near(q1)
        e0 = wide_shard(q1)
        ex0 = near(e0)
        qx3 = near(q3)
        qx2 = near(q2)
        w_pieces = [shard, q1, q3, q2, qx0, qx1, qx3, qx2]
        t_three = swap_core(t_two)
        e1 = along(e0, 1)
        e3 = along(e0, 3)
        ex1 = near(e1)
        s0 = after(low_shard, q3)
        sx0 = near(s0)
        e2 = along(e0, 2)
        w_pieces[-1] = after(qx2, e1)
    else:
        w_pieces = gather_whole(shard, count, HEADER)
        inputs = jnp.concatenate([inputs, marks], axis=1)
        t_two = across(inputs)
        t_one = swap_core(inputs)
        t_three = swap_core(t_two)
        e_pieces = gather_whole(wide_shard(shard), count, 0)
        sh_pieces = gather_whole(low_shard, count, 0)

    tok, w, wm, vec, qp, kp, v, q_t, k_t, o_t, lse, keep, send = call(
        partial(attend_kernel, parts_in),
        "attend",
        [
            ((length, width + 128), LOW),
            ((width, 640), LOW),
            ((width, half), LOW),
            ((HEADER, 640 + half), FULL),
            ((length, 256), LOW),
            ((length, 256), LOW),
            ((length, 256), LOW),
            ((256, length), LOW),
            ((256, length), LOW),
            ((slim, length), FULL),
            ((8, length), FULL),
            ((slim, near_rows), LOW),
            ((slim, near_rows), LOW),
        ],
        table,
        inputs,
        t_one,
        t_two,
        t_three,
        *w_pieces,
        scratch=[((3, length, 256), LOW), ((256, length), LOW)],
        flops=14e9,
        nbytes=1e7,
    )
    a_two = across(send)
    a_one = swap_core(keep)
    wm_other = swap_core(wm)
    a_three = swap_core(a_two)
    cot = cotangent.reshape(rows, width)
    cot_other = swap_core(after(cot, keep))
    if ring:
        ex3 = near(e3, keep)
        s1 = along(s0, 1, keep)
        ex2 = near(e2)
        s3 = along(s0, 3)
        s2 = along(s0, 2)
        sx1 = near(s1)
        sx3 = near(s3)
        sx2 = near(s2)
        e_pieces = [e0, e1, e3, e2, ex0, ex1, ex3, ex2]
        sh_pieces = [s0, s1, s3, s2, sx0, sx1, sx3, sx2]

    att, normed, rstd, low, e_bias = call(
        merge_kernel,
        "merge",
        [
            ((width, near_rows), LOW),
            ((near_rows, width), FULL),
            ((near_rows, 128), FULL),
            ((near_rows, width), LOW),
            ((EXTRA, hidden // 2), FULL),
        ],
        table,
        keep,
        a_one,
        a_two,
        a_three,
        tok,
        vec,
        wm,
        wm_other,
        scratch=[((near_rows, width), FULL)],
        flops=5e9,
        nbytes=1e7,
    )
    if ring:
        e_pieces[-1] = after(e_pieces[-1], low)
    e, act, slope = call(
        partial(gelu_kernel, parts_in),
        "gelu",
        [
            ((width, hidden // 2), LOW),
            ((near_rows, hidden // 2), LOW),
            ((near_rows, hidden // 2), LOW),
        ],
        table,
        low,
        e_bias,
        *e_pieces,
        flops=8e9,
        nbytes=1e7,
    )
    sh, part = call(
        partial(shrink_kernel, parts_in),
        "shrink",
        [((hidden // 2, width), LOW), ((near_rows, width), LOW)],
        table,
        act,
        *sh_pieces,
        flops=4e9,
        nbytes=1e7,
    )
    part_other = swap_core(part)
    out, dsec, dz, sums_two = call(
        second_kernel,
        "second",
        [
            ((rows, width), LOW),
            ((near_rows, width), FULL),
            ((near_rows, width), LOW),
            ((EXTRA, width), FULL),
        ],
        table,
        normed,
        vec,
        part,
        part_other,
        cot,
        cot_other,
        scratch=[((near_rows, width), FULL)],
        flops=5e9,
        nbytes=8e6,
    )
    sh_blocks = call(
        partial(shrink_grad_kernel, parts),
        "shrink_grad",
        [((parts // 4, hidden // 2 // parts, width), LOW)] * 4,
        table,
        act,
        dz,
        scratch=[((hidden // 2, width), LOW)],
        flops=5e9,
        nbytes=5e6,
    )
    dpre, dfp, sums_hid = call(
        hidden_kernel,
        "hidden",
        [
            ((near_rows, hidden // 2), LOW),
            ((near_rows, width), LOW),
            ((EXTRA, hidden // 2), FULL),
        ],
        table,
        after(dz, sh_blocks[0]),
        slope,
        e,
        sh,
        flops=6e9,
        nbytes=8e6,
    )
    dfp_other = swap_core(dfp)
    dres, dbr, dkeep, dsend, sums_one = call(
        first_kernel,
        "first",
        [
            ((rows, width), FULL),
            ((near_rows, width), LOW),
            ((slim, near_rows), LOW),
            ((slim, near_rows), LOW),
            ((EXTRA, width), FULL),
        ],
        table,
        dfp,
        dfp_other,
        dsec,
        normed,
        rstd,
        vec,
        wm,
        wm_other,
        scratch=[((near_rows, width), FULL)],
        flops=5e9,
        nbytes=8e6,
    )
    dother = across(dsend)
    em_blocks = call(
        partial(expand_grad_kernel, parts),
        "expand_grad",
        [((parts // 4, width // parts + EXTRA, half + hidden // 2), LOW)] * 4,
        table,
        low,
        dpre,
        att,
        dbr,
        sums_two,
        sums_hid,
        sums_one,
        scratch=[((width, half + hidden // 2), LOW), ((EXTRA, half + hidden // 2), FULL)],
        flops=5e9,
        nbytes=8e6,
    )
    def finish_half(blocks, got, i):
        if i == 0:
            p2, p1 = pair_sum(blocks[2], got)
            return along(p2, 2), along(p1, 1), p1
        p3, p0 = pair_sum(blocks[3], got)
        return along(p3, 3), p0

    if ring:
        sh_got = [near(sh_blocks[0]), near(sh_blocks[1])]
        em_got = [near(em_blocks[0])]
        r2, r1, mark = finish_half(sh_blocks, after(sh_got[0], em_blocks[0]), 0)
        sh_sums = [r2, r1]
        gate = mark
    else:
        gate = em_blocks[0]
    *w_blocks, grads = call(
        partial(attend_back_kernel, parts),
        "attend_back",
        [((parts // 4, width // parts + EXTRA, 640), LOW)] * 4 + [((length, 640), LOW)],
        table,
        tok,
        qp,
        kp,
        v,
        q_t,
        k_t,
        o_t,
        lse,
        dkeep,
        after(dother, gate),
        scratch=[
            ((length, 3 * length), LOW),
            ((length, 3 * length), LOW),
            ((256, length), LOW),
            ((3 * length, 256), LOW),
            ((3 * length, 256), LOW),
            ((3, length, 256), LOW),
            ((3, length, 256), LOW),
            ((256, length), FULL),
            ((width, 640), LOW),
        ],
        flops=16e9,
        nbytes=1e7,
    )
    if ring:
        sh_sums += list(finish_half(sh_blocks, after(sh_got[1], grads), 1))
        gate = sh_sums[-1]
    else:
        gate = w_blocks[0]
    x_send, x_keep = call(
        input_grad_kernel,
        "input_grad",
        [((2, rows, width), LOW)] * 2,
        table,
        after(grads, gate),
        w,
        scratch=[((length, width), LOW)],
        flops=4e9,
        nbytes=5e6,
    )
    x_sum = x_keep.astype(FULL) + swap_core(x_send).astype(FULL)
    x_other = across(x_sum[1].astype(LOW))
    in_grad = dres + x_sum[0] + x_other.astype(FULL)


    if ring:
        em_got.append(near(em_blocks[1]))
        r2, r1, mark = finish_half(em_blocks, after(em_got[0], x_send), 0)
        em_sums = [r2, r1]
        w_got = [near(w_blocks[0])]
        em_sums += list(finish_half(em_blocks, after(em_got[1], mark), 1))
        w_got.append(near(w_blocks[1]))
        r2, r1, mark = finish_half(w_blocks, after(w_got[0], em_sums[-1]), 0)
        w_sums = [r2, r1] + list(finish_half(w_blocks, after(w_got[1], mark), 1))
        shrink_own, em_own, w_own = [
            g[0].astype(FULL) + g[1].astype(FULL) + g[2].astype(FULL) + g[3].astype(FULL)
            for g in (sh_sums, em_sums, w_sums)
        ]
    else:
        shrink_own, em_own, w_own = [
            scatter_whole(
                jnp.concatenate(g[:2], axis=0), jnp.concatenate(g[2:], axis=0), count, extra
            )
            for g, extra in ((sh_blocks, 0), (em_blocks, EXTRA), (w_blocks, EXTRA))
        ]
    w_own = w_own.astype(LOW)

    def over_chips(part):
        part = part.astype(LOW)
        return part.astype(FULL) + across(part).astype(FULL)

    def both_cores(part):
        other = swap_core(part)
        return jnp.where(c == 0, part, other), jnp.where(c == 0, other, part)

    sh_low, sh_high = both_cores(over_chips(shrink_own))
    d_shrink = jnp.concatenate([sh_low, sh_high], axis=0)
    em_own = over_chips(em_own)
    w_two = across(w_own)
    w_one = swap_core(w_own)
    w_three = swap_core(w_two)
    em_other = swap_core(em_own)
    d_merge, d_expand, em_rows = final_wide(
        ring, table, c, em_own, em_other, share, half, hidden, unit, count
    )
    small = lax.dynamic_slice(em_rows[0], (0, share * own), (6, share))
    d_b_expand = jnp.concatenate(
        [
            lax.dynamic_slice(em_rows[i], (6, unit * own), (1, unit)).reshape(unit)
            for i in range(2)
        ]
    )
    d_q, d_k, d_v, w_rows = call(
        final_projection_kernel,
        "final_projection",
        [((share, width), FULL)] * 3 + [((16, width), FULL)],
        table,
        w_own,
        w_one,
        w_two,
        w_three,
        scratch=[((4, share + EXTRA, 640), FULL)],
    )
    w_rows = lax.dynamic_slice(w_rows, (0, share * own), (16, share))

    return (
        out.reshape(1, rows, width),
        in_grad.astype(LOW).reshape(1, rows, width),
        d_q,
        d_k,
        d_v,
        d_merge,
        w_rows[0],
        w_rows[8],
        small[0],
        small[1],
        small[2],
        d_expand,
        d_b_expand,
        d_shrink,
        small[3],
        small[4],
        small[5],
    )


def final_wide(ring, table, c, mine, theirs, share, half, hidden, unit, count):
    if ring:
        return call(
            final_wide_kernel,
            "final_wide",
            [
                ((share, 2 * half), FULL),
                ((share, hidden), FULL),
                ((2, EXTRA, half + hidden // 2), FULL),
            ],
            table,
            mine,
            theirs,
            scratch=[((2, share + EXTRA, half + hidden // 2), FULL)],
        )
    low, high = jnp.where(c == 0, mine, theirs), jnp.where(c == 0, theirs, mine)
    merge = jnp.concatenate([low[:share, :half], high[:share, :half]], axis=1)
    wide = jnp.stack(
        [part[:share, half:].reshape(share, count, unit) for part in (low, high)], axis=2
    ).reshape(share, hidden)
    return merge, wide, jnp.stack([low[share:], high[share:]])


def solution(mesh):
    row, flat = P("fsdp", None), P("fsdp")
    cube = P("fsdp", "seq", None)
    return jax.shard_map(
        partial(body, mesh.shape["fsdp"]),
        mesh=mesh,
        in_specs=(cube, P("fsdp", "seq"))
        + (row,) * 4
        + (flat,) * 5
        + (row, flat, row)
        + (flat,) * 3
        + (cube,),
        out_specs=(cube, cube) + (row,) * 4 + (flat,) * 5 + (row, flat, row) + (flat,) * 3,
        check_vma=False,
    )
```

```python
from functools import partial

import jax
import jax.numpy as jnp
from jax import lax
from jax.experimental import pallas as pl
from jax.experimental.pallas import tpu as pltpu
from jax.sharding import PartitionSpec as P

HEAD_DIM = 64
LOW = jnp.bfloat16
FULL = jnp.float32
VMEM = pl.BlockSpec(memory_space=pltpu.VMEM)
SMEM = pl.BlockSpec(memory_space=pltpu.SMEM)
CORE_PAIRS = [(0, 1), (1, 0), (2, 3), (3, 2)]
CHIP_PAIRS = [(0, 2), (2, 0), (1, 3), (3, 1)]
EXTRA = 8
HEADER = 16
FAR = -1e9


def nn(a, b):
    return lax.dot_general(a, b, (((1,), (0,)), ((), ())), preferred_element_type=FULL)


def nt(a, b):
    return lax.dot_general(a, b, (((1,), (1,)), ((), ())), preferred_element_type=FULL)


def tn(a, b):
    return lax.dot_general(a, b, (((0,), (0,)), ((), ())), preferred_element_type=FULL)


def rows_at(block, size):
    return pl.ds(pl.multiple_of(block * size, size), size)


def call(kernel, name, outs, table, *args, scratch=(), flops=0, nbytes=0):
    return pl.pallas_call(
        kernel,
        name=name,
        out_shape=[jax.ShapeDtypeStruct(shape, dtype) for shape, dtype in outs],
        in_specs=[SMEM] + [VMEM] * len(args),
        out_specs=[VMEM] * len(outs),
        scratch_shapes=[pltpu.VMEM(shape, dtype) for shape, dtype in scratch],
        cost_estimate=pl.CostEstimate(
            flops=0, bytes_accessed=0, transcendentals=0
        ),
    )(table, *args)


def attend_kernel(parts, table, t0, t1, t2, t3, *refs):
    pieces, refs = refs[:parts], refs[parts:]
    tok, w, wm, vec, qp, kp, v, q_t, k_t, o_t, lse, keep, send, heads, v_t = refs
    seq, y = table[0], table[1]
    rows = t0.shape[0]
    width = w.shape[0]
    piece = width // parts
    length = tok.shape[0]
    for j, t in enumerate((t0, t1, t2, t3)):
        tok[rows_at(seq ^ j, rows), :] = t[...]
    total = jnp.zeros(vec.shape, FULL)
    for p, ref in enumerate(pieces):
        at = rows_at(table[4 + p], piece)
        w[at, :] = ref[:piece, :640]
        wm[at, :] = ref[:piece, 640:]
        total = total + ref[piece : piece + HEADER, :].astype(FULL)
    vec[...] = total
    bias = vec[8:9, :640]
    lane = lax.broadcasted_iota(jnp.int32, (rows, 256), 1)
    mark = (lane - 192).astype(FULL)
    for i in range(length // rows):
        here = slice(i * rows, (i + 1) * rows)
        x = nn(tok[here, :width], w[...]) + bias
        seg = tok[here, width : width + 128].astype(FULL)
        seg = jnp.concatenate([seg, seg], axis=1)
        q = x[:, :256].astype(LOW).astype(FULL) * 0.125
        q = jnp.where(lane < 192, q, jnp.where((lane < 196) & (mark != seg), FAR, 0.0))
        k = pltpu.roll(x[:, 128:384], 192, 1).astype(LOW).astype(FULL)
        k = jnp.where(lane < 192, k, jnp.where(mark == seg, 1.0, 0.0))
        vv = x[:, 384:640]
        qp[here, :] = q.astype(LOW)
        kp[here, :] = k.astype(LOW)
        v[here, :] = vv.astype(LOW)
        q_t[:, here] = q.T.astype(LOW)
        k_t[:, here] = k.T.astype(LOW)
        v_t[:, here] = vv.T.astype(LOW)
        for h in range(3):
            heads[h, here, :] = jnp.where(
                (lane // HEAD_DIM == h) | (lane >= 192), k, 0.0
            ).astype(LOW)
    lse[...] = jnp.zeros(lse.shape, FULL)

    @pl.loop(0, length // 256)
    def _(i):
        cols = rows_at(i, 256)
        for h in range(3):
            mine = slice(HEAD_DIM * h, HEAD_DIM * (h + 1))
            scores = nn(heads[h], q_t[:, cols])
            top = jnp.max(scores, axis=0, keepdims=True)
            expo = jnp.exp(scores - top)
            total = jnp.sum(expo, axis=0, keepdims=True)
            mixed = nn(v_t[mine, :], expo.astype(LOW))
            o_t[mine, cols] = mixed * (1.0 / total)
            lse[h : h + 1, cols] = top + jnp.log(total)

    half = length // 2
    keep[...] = o_t[:, rows_at(y, half)].astype(LOW)
    send[...] = o_t[:, rows_at(1 - y, half)].astype(LOW)


def gelu_parts(u):
    phi = 0.5 + 0.5 * lax.erf(u * 0.7071067811865476)
    bell = jnp.exp(-0.5 * u * u)
    return u * phi, phi + u * (bell * 0.3989422804014327)


def merge_kernel(table, a0, a1, a2, a3, tok, vec, mine, theirs, att, normed, rstd, low, bias, work):
    seq, y, c = table[0], table[1], table[2]
    count, width = normed.shape
    half = width // 2
    for j, a in enumerate((a0, a1, a2, a3)):
        att[rows_at(seq ^ j, 192), :] = a[...]
    bias[...] = jnp.broadcast_to(
        jnp.concatenate([vec[6:7, :width], vec[7:8, :width]], axis=1), bias.shape
    )
    work[:, rows_at(c, half)] = tn(att[...], mine[...])
    work[:, rows_at(1 - c, half)] = tn(att[...], theirs[...])
    values = tok[rows_at(y, count), :width].astype(FULL) + work[...] + vec[0:1, :width]
    center = values - jnp.mean(values, axis=1, keepdims=True)
    scale = lax.rsqrt(jnp.mean(center * center, axis=1, keepdims=True) + 1e-12)
    center = center * scale
    normed[...] = center
    rstd[...] = jnp.broadcast_to(scale, rstd.shape)
    low[...] = (center * vec[1:2, :width] + vec[2:3, :width]).astype(LOW)


def gelu_kernel(parts, table, low, bias, *refs):
    pieces, (e, act, slope) = refs[:parts], refs[parts:]
    piece = e.shape[0] // parts
    for p, ref in enumerate(pieces):
        e[rows_at(table[4 + p], piece), :] = ref[...]

    @pl.loop(0, act.shape[1] // 256)
    def _(i):
        cols = rows_at(i, 256)
        pre = nn(low[...], e[:, cols]) + bias[0:1, cols]
        value, grad = gelu_parts(pre)
        act[:, cols] = value.astype(LOW)
        slope[:, cols] = grad.astype(LOW)


def shrink_kernel(parts, table, act, *refs):
    pieces, (sh, part) = refs[:parts], refs[parts:]
    piece = sh.shape[0] // parts
    for p, ref in enumerate(pieces):
        sh[rows_at(table[4 + p], piece), :] = ref[...]
    part[...] = nn(act[...], sh[...]).astype(LOW)


def second_kernel(table, normed, vec, mine, theirs, cot_mine, cot_theirs, *refs):
    out, dsec, dz, sums, work = refs
    c = table[2]
    rows = cot_mine.shape[0]
    width = normed.shape[1]
    first = normed[...] * vec[1:2, :width] + vec[2:3, :width]
    second = first + (mine[...].astype(FULL) + theirs[...].astype(FULL)) + vec[3:4, :width]
    center = second - jnp.mean(second, axis=1, keepdims=True)
    scale = lax.rsqrt(jnp.mean(center * center, axis=1, keepdims=True) + 1e-12)
    center = center * scale
    gain = vec[4:5, :width]
    work[...] = center * gain + vec[5:6, :width]
    out[...] = work[rows_at(c, rows), :].astype(LOW)
    work[rows_at(c, rows), :] = cot_mine[...].astype(FULL)
    work[rows_at(1 - c, rows), :] = cot_theirs[...].astype(FULL)
    up = work[...]
    sums[...] = jnp.zeros(sums.shape, FULL)
    sums[0:1, :] = jnp.sum(up * center, axis=0, keepdims=True)
    sums[1:2, :] = jnp.sum(up, axis=0, keepdims=True)
    scaled = up * gain
    grad = scale * (
        scaled
        - jnp.mean(scaled, axis=1, keepdims=True)
        - center * jnp.mean(scaled * center, axis=1, keepdims=True)
    )
    dsec[...] = grad
    dz[...] = grad.astype(LOW)
    sums[2:3, :] = jnp.sum(dz[...].astype(FULL), axis=0, keepdims=True)


def hidden_kernel(table, dz, slope, e, sh, dpre, dfp, sums):
    hidden = sh.shape[0]
    sums[...] = jnp.zeros(sums.shape, FULL)

    @pl.loop(0, hidden // 256)
    def _(i):
        cols = rows_at(i, 256)
        value = nt(dz[...], sh[cols, :]) * slope[:, cols].astype(FULL)
        value = value.astype(LOW)
        dpre[:, cols] = value
        sums[0:1, cols] = jnp.sum(value.astype(FULL), axis=0, keepdims=True)

    dfp[...] = nt(dpre[...], e[...]).astype(LOW)


def put_blocks(parts, table, work, block, outs, extra=None):
    for i, ref in enumerate(outs):
        for j in range(parts // 4):
            at = table[4 + parts + i * (parts // 4) + j]
            ref[j, :block, :] = work[rows_at(at, block), :]
            if extra is not None:
                ref[j, block:, :] = extra


def shrink_grad_kernel(parts, table, act, dz, *refs):
    outs, work = refs[:4], refs[4]
    work[...] = tn(act[...], dz[...]).astype(LOW)
    put_blocks(parts, table, work, work.shape[0] // parts, outs)


def first_kernel(
    table, mine, theirs, dsec, normed, rstd, vec, wm, wm_other, dres, dbr, dkeep, dsend, sums, work
):
    seq, c = table[0], table[2]
    width = normed.shape[1]
    half = width // 2
    rows = dres.shape[0]
    up = (mine[...].astype(FULL) + theirs[...].astype(FULL)) + dsec[...]
    center = normed[...]
    sums[...] = jnp.zeros(sums.shape, FULL)
    sums[0:1, :] = jnp.sum(up * center, axis=0, keepdims=True)
    sums[1:2, :] = jnp.sum(up, axis=0, keepdims=True)
    scaled = up * vec[1:2, :width]
    work[...] = rstd[:, 0:1] * (
        scaled
        - jnp.mean(scaled, axis=1, keepdims=True)
        - center * jnp.mean(scaled * center, axis=1, keepdims=True)
    )
    dbr[...] = work[...].astype(LOW)
    dres[...] = work[rows_at(c, rows), :]
    sums[2:3, :] = jnp.sum(dbr[...].astype(FULL), axis=0, keepdims=True)
    for j, ref in ((0, dkeep), (2, dsend)):
        at = rows_at(seq ^ j, 192)
        ref[...] = (
            nt(wm[at, :], dbr[:, rows_at(c, half)])
            + nt(wm_other[at, :], dbr[:, rows_at(1 - c, half)])
        ).astype(LOW)


def expand_grad_kernel(parts, table, low, dpre, att, dbr, sums_two, sums_hid, sums_one, *refs):
    outs, (work, rows) = refs[:4], refs[4:]
    c = table[2]
    width = low.shape[1]
    half = width // 2
    work[:, :half] = nn(att[...], dbr[:, rows_at(c, half)]).astype(LOW)
    work[:, half:] = tn(low[...], dpre[...]).astype(LOW)
    rows[...] = jnp.zeros(rows.shape, FULL)
    rows[0:1, :width] = sums_one[2:3, :]
    rows[1:3, :width] = sums_one[0:2, :]
    rows[3:4, :width] = sums_two[2:3, :]
    rows[4:6, :width] = sums_two[0:2, :]
    rows[6:7, : dpre.shape[1]] = sums_hid[0:1, :]
    put_blocks(parts, table, work, width // parts, outs, rows[...].astype(LOW))


def attend_back_kernel(
    parts, table, tok, qp, kp, v, q_t, k_t, o_t, lse, dkeep, dother, *refs
):
    outs, refs = refs[:4], refs[4:]
    grads, probs, dscores, d_t, d_rows, q_rows, heads, v_heads, dq_t, work = refs
    y = table[1]
    length = tok.shape[0]
    width = work.shape[0]
    block = width // parts
    half = length // 2
    d_t[192:, :] = jnp.zeros((64, length), LOW)
    d_t[:192, rows_at(y, half)] = dkeep[...]
    d_t[:192, rows_at(1 - y, half)] = dother[...]
    lane = lax.broadcasted_iota(jnp.int32, (256, 256), 1)
    for i in range(length // 256):
        here = slice(i * 256, (i + 1) * 256)
        d = d_t[:, here].astype(FULL).T
        k = kp[here, :].astype(FULL)
        q = qp[here, :].astype(FULL)
        vv = v[here, :].astype(FULL)
        for h in range(3):
            own = lane // HEAD_DIM == h
            at = slice(h * length + i * 256, h * length + (i + 1) * 256)
            d_rows[at, :] = jnp.where(own, d, 0.0).astype(LOW)
            q_rows[at, :] = jnp.where(own, q, 0.0).astype(LOW)
            heads[h, here, :] = jnp.where(own | (lane >= 192), k, 0.0).astype(LOW)
            v_heads[h, here, :] = jnp.where(own, vv, 0.0).astype(LOW)
    dq_t[192:, :] = jnp.zeros((64, length), FULL)

    @pl.loop(0, length // 256)
    def _(i):
        cols = rows_at(i, 256)
        for h in range(3):
            mine = slice(HEAD_DIM * h, HEAD_DIM * (h + 1))
            out = pl.ds(pl.multiple_of(h * length + i * 256, 256), 256)
            prob = jnp.exp(nn(heads[h], q_t[:, cols]) - lse[h : h + 1, cols])
            probs[:, out] = prob.astype(LOW)
            delta = jnp.sum(
                d_t[mine, cols].astype(FULL) * o_t[mine, cols], axis=0, keepdims=True
            )
            grad = (prob * (nn(v_heads[h], d_t[:, cols]) - delta)).astype(LOW)
            dscores[:, out] = grad
            dq_t[mine, cols] = nn(k_t[mine, :], grad) * 0.125

    for i in range(length // 256):
        here = slice(i * 256, (i + 1) * 256)
        dv = nn(probs[here, :], d_rows[...])
        dk = pltpu.roll(nn(dscores[here, :], q_rows[...]), 192, 1)
        dq = dq_t[:, here].T
        grads[here, :256] = jnp.where(lane < 192, dq, dk).astype(LOW)
        grads[here, 256:384] = dk[:, :128].astype(LOW)
        grads[here, 384:] = dv.astype(LOW)
    work[...] = tn(tok[:, :width], grads[...]).astype(LOW)
    total = jnp.sum(grads[...].astype(FULL), axis=0, keepdims=True)
    total = jnp.broadcast_to(total, (EXTRA, total.shape[1])).astype(LOW)
    put_blocks(parts, table, work, block, outs, total)


def input_grad_kernel(table, grads, w, send, keep, work):
    seq = table[0]
    rows = send.shape[1]
    work[...] = nt(grads[...], w[...]).astype(LOW)
    for b in range(2):
        send[b] = work[rows_at(seq ^ (1 + 2 * b), rows), :]
        keep[b] = work[rows_at(seq ^ (2 * b), rows), :]


def pair_kernel(keep, got, *outs):
    for k, ref in enumerate(outs):
        ref[...] = (keep[k].astype(FULL) + got[k].astype(FULL)).astype(LOW)


def projection_kernel(table, wq, wk, wv, merge, rest, out):
    seq, c = table[0], table[2]
    share, width = wq.shape
    slim, half = width // 4, width // 2
    for s in range(4):

        @pl.when(seq == s)
        def _():
            cols = slice(slim * s, slim * (s + 1))
            for i, ref in enumerate((wq, wk, wv)):
                out[:share, slim * i : slim * (i + 1)] = ref[:, cols]

    out[:share, 3 * slim : 640] = jnp.zeros((share, 640 - 3 * slim), LOW)
    out[:share, 640:] = merge[:, rows_at(c, half)]
    out[share:, :] = rest[...]


def wide_kernel(unit, table, wide, out):
    c = table[2]
    for s in range(2):

        @pl.when(c == s)
        def _():
            for f in range(out.shape[1] // unit):
                start = 2 * unit * f + unit * s
                out[:, unit * f : unit * (f + 1)] = wide[:, start : start + unit]


def final_projection_kernel(table, p0, p1, p2, p3, dq, dk, dv, rows, stack):
    seq = table[0]
    share = dq.shape[0]
    slim = dq.shape[1] // 4
    for j, p in enumerate((p0, p1, p2, p3)):
        stack[j] = p[...].astype(FULL)
    for i in range(4):
        part = stack[seq ^ i]
        cols = slice(slim * i, slim * (i + 1))
        for g, ref in enumerate((dq, dk, dv)):
            ref[:, cols] = part[:share, slim * g : slim * (g + 1)]
            if g != 1:
                rows[4 * g : 4 * g + 8, cols] = part[share : share + 8, slim * g : slim * (g + 1)]


def final_wide_kernel(table, mine, theirs, merge, wide, rows, both):
    c = table[2]
    share, half = merge.shape[0], merge.shape[1] // 2
    hidden = wide.shape[1]
    unit = hidden // 16
    both[c] = mine[...]
    both[1 - c] = theirs[...]
    for s in range(2):
        merge[:, half * s : half * (s + 1)] = both[s, :share, :half]
        for f in range(8):
            start = half + unit * f
            at = 2 * unit * f + unit * s
            wide[:, at : at + unit] = both[s, :share, start : start + unit]
        rows[s] = both[s, share:, :]


def after(x, *others):
    return lax.optimization_barrier((x,) + others)[0]


class Link:
    def __init__(self, window=2):
        self.window = window
        self.done = []

    def send(self, x, axis, pairs, *others, free=False):
        if len(self.done) >= self.window and not free:
            others = others + (self.done[-self.window],)
        if others:
            x = after(x, *others)
        self.done.append(lax.ppermute(x, axis, pairs))
        return self.done[-1]


NEAR_PAIRS = [(i, i ^ 1) for i in range(8)]
SHIFTS = {k: [(i, (i + 2 * k) % 8) for i in range(8)] for k in (1, 2, 3)}


def swap_core(x):
    return lax.ppermute(x, "seq", CORE_PAIRS)


def gather_whole(shard, count, extra):
    whole = lax.all_gather(shard, "fsdp", axis=0)
    rows = shard.shape[0] - extra
    main = whole[:, :rows].reshape(count * rows, shard.shape[1])
    if not extra:
        return [main]
    rest = jnp.sum(whole[:, rows:].astype(FULL), axis=0).astype(LOW)
    return [jnp.concatenate([main, rest], axis=0)]


def scatter_whole(send, keep, count, extra):
    both = jnp.concatenate([send, keep], axis=0)
    rows = both.shape[1] - extra
    main = both[:, :rows].reshape(count, -1, both.shape[2])
    rest = jnp.broadcast_to(both[:1, rows:], (count, extra, both.shape[2]))
    both = jnp.concatenate([main, rest], axis=1)
    return lax.psum_scatter(both, "fsdp", scatter_dimension=0).astype(FULL)


def pair_sum(keep, got):
    shape = keep.shape[1:]
    return pl.pallas_call(
        pair_kernel,
        name="pair",
        out_shape=[jax.ShapeDtypeStruct(shape, LOW)] * keep.shape[0],
        in_specs=[VMEM, VMEM],
        out_specs=[VMEM] * keep.shape[0],
        cost_estimate=pl.CostEstimate(
            flops=0, bytes_accessed=0, transcendentals=0
        ),
    )(keep, got)


def body(
    count,
    tokens,
    segment_ids,
    query_weight,
    key_weight,
    value_weight,
    merge_weight,
    query_bias,
    value_bias,
    merge_bias,
    first_gain,
    first_shift,
    expand_weight,
    expand_bias,
    shrink_weight,
    shrink_bias,
    second_gain,
    second_shift,
    cotangent,
):
    rows, width = tokens.shape[1:]
    hidden = expand_weight.shape[1]
    share = width // count
    unit = hidden // count // 2
    slim = width // 4
    half = width // 2
    length = 4 * rows
    near_rows = 2 * rows
    seq = lax.axis_index("seq")
    own = lax.axis_index("fsdp")
    c, y = seq % 2, seq // 2
    z, x = own // 2, own % 2
    ring = count == 8
    if ring:
        parts = parts_in = 8
        mine = [((z - k) % 4) * 2 + x for k in (0, 1, 3, 2)]
        pieces = mine + [2 * (m // 2) + 1 - x for m in mine]
        there = [2 * ((z + k) % 4) for k in (2, 1, 3, 0)]
        blocks = [t + 1 - x for t in there] + [t + x for t in there]
    else:
        parts, parts_in = 4, 1
        pieces, blocks = [0], [0, 1, 2, 3]
    pieces = pieces + [0] * (parts - parts_in)
    table = jnp.stack([seq, y, c, z] + pieces + blocks).astype(jnp.int32)
    x_link, y_link, z_link = Link(), Link(), Link()

    def near(v, *others, free=False):
        return x_link.send(v, "fsdp", NEAR_PAIRS, *others, free=free)

    def along(v, k, *others, free=False):
        return z_link.send(v, "fsdp", SHIFTS[k], *others, free=free)

    def across(v, *others):
        return y_link.send(v, "seq", CHIP_PAIRS, *others)

    pair = jnp.stack([query_bias, value_bias])
    pair = lax.dynamic_update_slice(jnp.zeros((2, width), LOW), pair, (0, share * own))
    pair = lax.dynamic_slice(pair, (0, slim * seq), (2, slim))
    bias_row = jnp.concatenate([pair[0:1], jnp.zeros((1, slim), LOW), pair[1:2]], axis=1)
    rest = jnp.zeros((HEADER, 640 + half), LOW)
    stack = jnp.stack(
        [merge_bias, first_gain, first_shift, shrink_bias, second_gain, second_shift]
    )
    rest = lax.dynamic_update_slice(rest, stack, (0, share * own))
    chunk = lax.dynamic_slice(expand_bias, (unit * c,), (unit,)).reshape(1, unit)
    rest = lax.dynamic_update_slice(
        rest, chunk, (6 + unit * own // width, unit * own % width)
    )
    rest = lax.dynamic_update_slice(rest, bias_row, (8, 0))
    (shard,) = call(
        projection_kernel,
        "projection",
        [((share + HEADER, 640 + half), LOW)],
        table,
        query_weight,
        key_weight,
        value_weight,
        merge_weight,
        rest,
    )
    inputs = tokens.reshape(rows, width)
    marks = jnp.broadcast_to(segment_ids.reshape(rows, 1).astype(LOW), (rows, 128))

    def wide_shard(dep):
        weight = after(expand_weight, dep)
        if ring:
            return call(
                partial(wide_kernel, unit),
                "wide",
                [((share, hidden // 2), LOW)],
                table,
                weight,
            )[0]
        wide = weight.reshape(share, count, 2, unit)
        return jnp.where(c == 0, wide[:, :, 0], wide[:, :, 1]).reshape(share, hidden // 2)

    low_shard = lax.dynamic_slice(shrink_weight, (unit * c, 0), (unit, width))
    if ring:
        q1 = along(shard, 1)
        q3 = along(shard, 3)
        q2 = along(shard, 2)
        qx0 = near(shard)
        inputs = jnp.concatenate([inputs, marks], axis=1)
        t_two = across(inputs)
        t_one = swap_core(inputs)
        qx1 = near(q1)
        e0 = wide_shard(q1)
        ex0 = near(e0)
        qx3 = near(q3)
        qx2 = near(q2)
        w_pieces = [shard, q1, q3, q2, qx0, qx1, qx3, qx2]
        t_three = swap_core(t_two)
        e1 = along(e0, 1)
        e3 = along(e0, 3)
        ex1 = near(e1)
        s0 = after(low_shard, q3)
        sx0 = near(s0)
        e2 = along(e0, 2)
        w_pieces[-1] = after(qx2, e1)
    else:
        w_pieces = gather_whole(shard, count, HEADER)
        inputs = jnp.concatenate([inputs, marks], axis=1)
        t_two = across(inputs)
        t_one = swap_core(inputs)
        t_three = swap_core(t_two)
        e_pieces = gather_whole(wide_shard(shard), count, 0)
        sh_pieces = gather_whole(low_shard, count, 0)

    tok, w, wm, vec, qp, kp, v, q_t, k_t, o_t, lse, keep, send = call(
        partial(attend_kernel, parts_in),
        "attend",
        [
            ((length, width + 128), LOW),
            ((width, 640), LOW),
            ((width, half), LOW),
            ((HEADER, 640 + half), FULL),
            ((length, 256), LOW),
            ((length, 256), LOW),
            ((length, 256), LOW),
            ((256, length), LOW),
            ((256, length), LOW),
            ((slim, length), FULL),
            ((8, length), FULL),
            ((slim, near_rows), LOW),
            ((slim, near_rows), LOW),
        ],
        table,
        inputs,
        t_one,
        t_two,
        t_three,
        *w_pieces,
        scratch=[((3, length, 256), LOW), ((256, length), LOW)],
        flops=14e9,
        nbytes=1e7,
    )
    a_two = across(send)
    a_one = swap_core(keep)
    wm_other = swap_core(wm)
    a_three = swap_core(a_two)
    cot = cotangent.reshape(rows, width)
    cot_other = swap_core(after(cot, keep))
    if ring:
        ex3 = near(e3, keep)
        s1 = along(s0, 1, keep)
        ex2 = near(e2)
        s3 = along(s0, 3)
        s2 = along(s0, 2)
        sx1 = near(s1)
        sx3 = near(s3)
        sx2 = near(s2)
        e_pieces = [e0, e1, e3, e2, ex0, ex1, ex3, ex2]
        sh_pieces = [s0, s1, s3, s2, sx0, sx1, sx3, sx2]

    att, normed, rstd, low, e_bias = call(
        merge_kernel,
        "merge",
        [
            ((width, near_rows), LOW),
            ((near_rows, width), FULL),
            ((near_rows, 128), FULL),
            ((near_rows, width), LOW),
            ((EXTRA, hidden // 2), FULL),
        ],
        table,
        keep,
        a_one,
        a_two,
        a_three,
        tok,
        vec,
        wm,
        wm_other,
        scratch=[((near_rows, width), FULL)],
        flops=5e9,
        nbytes=1e7,
    )
    if ring:
        e_pieces[-1] = after(e_pieces[-1], low)
    e, act, slope = call(
        partial(gelu_kernel, parts_in),
        "gelu",
        [
            ((width, hidden // 2), LOW),
            ((near_rows, hidden // 2), LOW),
            ((near_rows, hidden // 2), LOW),
        ],
        table,
        low,
        e_bias,
        *e_pieces,
        flops=8e9,
        nbytes=1e7,
    )
    sh, part = call(
        partial(shrink_kernel, parts_in),
        "shrink",
        [((hidden // 2, width), LOW), ((near_rows, width), LOW)],
        table,
        act,
        *sh_pieces,
        flops=4e9,
        nbytes=1e7,
    )
    part_other = swap_core(part)
    out, dsec, dz, sums_two = call(
        second_kernel,
        "second",
        [
            ((rows, width), LOW),
            ((near_rows, width), FULL),
            ((near_rows, width), LOW),
            ((EXTRA, width), FULL),
        ],
        table,
        normed,
        vec,
        part,
        part_other,
        cot,
        cot_other,
        scratch=[((near_rows, width), FULL)],
        flops=5e9,
        nbytes=8e6,
    )
    sh_blocks = call(
        partial(shrink_grad_kernel, parts),
        "shrink_grad",
        [((parts // 4, hidden // 2 // parts, width), LOW)] * 4,
        table,
        act,
        dz,
        scratch=[((hidden // 2, width), LOW)],
        flops=5e9,
        nbytes=5e6,
    )
    dpre, dfp, sums_hid = call(
        hidden_kernel,
        "hidden",
        [
            ((near_rows, hidden // 2), LOW),
            ((near_rows, width), LOW),
            ((EXTRA, hidden // 2), FULL),
        ],
        table,
        after(dz, sh_blocks[0]),
        slope,
        e,
        sh,
        flops=6e9,
        nbytes=8e6,
    )
    dfp_other = swap_core(dfp)
    dres, dbr, dkeep, dsend, sums_one = call(
        first_kernel,
        "first",
        [
            ((rows, width), FULL),
            ((near_rows, width), LOW),
            ((slim, near_rows), LOW),
            ((slim, near_rows), LOW),
            ((EXTRA, width), FULL),
        ],
        table,
        dfp,
        dfp_other,
        dsec,
        normed,
        rstd,
        vec,
        wm,
        wm_other,
        scratch=[((near_rows, width), FULL)],
        flops=5e9,
        nbytes=8e6,
    )
    dother = across(dsend)
    em_blocks = call(
        partial(expand_grad_kernel, parts),
        "expand_grad",
        [((parts // 4, width // parts + EXTRA, half + hidden // 2), LOW)] * 4,
        table,
        low,
        dpre,
        att,
        dbr,
        sums_two,
        sums_hid,
        sums_one,
        scratch=[((width, half + hidden // 2), LOW), ((EXTRA, half + hidden // 2), FULL)],
        flops=5e9,
        nbytes=8e6,
    )
    def finish_half(blocks, got, i):
        if i == 0:
            p2, p1 = pair_sum(blocks[2], got)
            return along(p2, 2, free=True), along(p1, 1, free=True), p1
        p3, p0 = pair_sum(blocks[3], got)
        return along(p3, 3, free=True), p0

    if ring:
        sh_got = [near(sh_blocks[0], free=True), near(sh_blocks[1], free=True)]
        em_got = [near(em_blocks[0], sh_got[0], free=True)]
        r2, r1, mark = finish_half(sh_blocks, after(sh_got[0], em_blocks[0]), 0)
        sh_sums = [r2, r1]
        gate = mark
    else:
        gate = em_blocks[0]
    *w_blocks, grads = call(
        partial(attend_back_kernel, parts),
        "attend_back",
        [((parts // 4, width // parts + EXTRA, 640), LOW)] * 4 + [((length, 640), LOW)],
        table,
        tok,
        qp,
        kp,
        v,
        q_t,
        k_t,
        o_t,
        lse,
        dkeep,
        after(dother, gate),
        scratch=[
            ((length, 3 * length), LOW),
            ((length, 3 * length), LOW),
            ((256, length), LOW),
            ((3 * length, 256), LOW),
            ((3 * length, 256), LOW),
            ((3, length, 256), LOW),
            ((3, length, 256), LOW),
            ((256, length), FULL),
            ((width, 640), LOW),
        ],
        flops=16e9,
        nbytes=1e7,
    )
    if ring:
        sh_sums += list(finish_half(sh_blocks, after(sh_got[1], grads, r1, r2), 1))
        gate = sh_sums[-1]
    else:
        gate = w_blocks[0]
    x_send, x_keep = call(
        input_grad_kernel,
        "input_grad",
        [((2, rows, width), LOW)] * 2,
        table,
        after(grads, gate),
        w,
        scratch=[((length, width), LOW)],
        flops=4e9,
        nbytes=5e6,
    )
    x_sum = x_keep.astype(FULL) + swap_core(x_send).astype(FULL)
    x_other = across(x_sum[1].astype(LOW))
    in_grad = dres + x_sum[0] + x_other.astype(FULL)


    if ring:
        em_got.append(near(em_blocks[1], grads, free=True))
        r2, r1, mark = finish_half(em_blocks, after(em_got[0], x_send), 0)
        em_sums = [r2, r1]
        w_got = [near(w_blocks[0], em_got[1], free=True)]
        em_sums += list(finish_half(em_blocks, after(em_got[1], mark), 1))
        mark = em_sums[-1]
        w_got.append(near(w_blocks[1], mark, free=True))
        sh_sums[-1] = after(sh_sums[-1], mark)
        r2, r1, mark = finish_half(w_blocks, after(w_got[0], em_sums[-1]), 0)
        w_sums = [r2, r1] + list(finish_half(w_blocks, after(w_got[1], mark), 1))
        shrink_own, em_own, w_own = [
            g[0].astype(FULL) + g[1].astype(FULL) + g[2].astype(FULL) + g[3].astype(FULL)
            for g in (sh_sums, em_sums, w_sums)
        ]
    else:
        shrink_own, em_own, w_own = [
            scatter_whole(
                jnp.concatenate(g[:2], axis=0), jnp.concatenate(g[2:], axis=0), count, extra
            )
            for g, extra in ((sh_blocks, 0), (em_blocks, EXTRA), (w_blocks, EXTRA))
        ]
    w_own = w_own.astype(LOW)

    def over_chips(part):
        part = part.astype(LOW)
        return part.astype(FULL) + across(part).astype(FULL)

    def both_cores(part):
        other = swap_core(part)
        return jnp.where(c == 0, part, other), jnp.where(c == 0, other, part)

    sh_low, sh_high = both_cores(over_chips(shrink_own))
    d_shrink = jnp.concatenate([sh_low, sh_high], axis=0)
    em_own = over_chips(em_own)
    w_two = across(w_own)
    w_one = swap_core(w_own)
    w_three = swap_core(w_two)
    em_other = swap_core(em_own)
    d_merge, d_expand, em_rows = final_wide(
        ring, table, c, em_own, em_other, share, half, hidden, unit, count
    )
    small = lax.dynamic_slice(em_rows[0], (0, share * own), (6, share))
    d_b_expand = jnp.concatenate(
        [
            lax.dynamic_slice(em_rows[i], (6, unit * own), (1, unit)).reshape(unit)
            for i in range(2)
        ]
    )
    d_q, d_k, d_v, w_rows = call(
        final_projection_kernel,
        "final_projection",
        [((share, width), FULL)] * 3 + [((16, width), FULL)],
        table,
        w_own,
        w_one,
        w_two,
        w_three,
        scratch=[((4, share + EXTRA, 640), FULL)],
    )
    w_rows = lax.dynamic_slice(w_rows, (0, share * own), (16, share))

    return (
        out.reshape(1, rows, width),
        in_grad.astype(LOW).reshape(1, rows, width),
        d_q,
        d_k,
        d_v,
        d_merge,
        w_rows[0],
        w_rows[8],
        small[0],
        small[1],
        small[2],
        d_expand,
        d_b_expand,
        d_shrink,
        small[3],
        small[4],
        small[5],
    )


def final_wide(ring, table, c, mine, theirs, share, half, hidden, unit, count):
    if ring:
        return call(
            final_wide_kernel,
            "final_wide",
            [
                ((share, 2 * half), FULL),
                ((share, hidden), FULL),
                ((2, EXTRA, half + hidden // 2), FULL),
            ],
            table,
            mine,
            theirs,
            scratch=[((2, share + EXTRA, half + hidden // 2), FULL)],
        )
    low, high = jnp.where(c == 0, mine, theirs), jnp.where(c == 0, theirs, mine)
    merge = jnp.concatenate([low[:share, :half], high[:share, :half]], axis=1)
    wide = jnp.stack(
        [part[:share, half:].reshape(share, count, unit) for part in (low, high)], axis=2
    ).reshape(share, hidden)
    return merge, wide, jnp.stack([low[share:], high[share:]])


def solution(mesh):
    row, flat = P("fsdp", None), P("fsdp")
    cube = P("fsdp", "seq", None)
    return jax.shard_map(
        partial(body, mesh.shape["fsdp"]),
        mesh=mesh,
        in_specs=(cube, P("fsdp", "seq"))
        + (row,) * 4
        + (flat,) * 5
        + (row, flat, row)
        + (flat,) * 3
        + (cube,),
        out_specs=(cube, cube) + (row,) * 4 + (flat,) * 5 + (row, flat, row) + (flat,) * 3,
        check_vma=False,
    )
```

```python
from functools import partial

import jax
import jax.numpy as jnp
from jax import lax
from jax.experimental import pallas as pl
from jax.experimental.pallas import tpu as pltpu
from jax.sharding import PartitionSpec as P

HEAD_DIM = 64
LOW = jnp.bfloat16
FULL = jnp.float32
VMEM = pl.BlockSpec(memory_space=pltpu.VMEM)
SMEM = pl.BlockSpec(memory_space=pltpu.SMEM)
CORE_PAIRS = [(0, 1), (1, 0), (2, 3), (3, 2)]
CHIP_PAIRS = [(0, 2), (2, 0), (1, 3), (3, 1)]
EXTRA = 8
HEADER = 16
FAR = -1e9


def nn(a, b):
    return lax.dot_general(a, b, (((1,), (0,)), ((), ())), preferred_element_type=FULL)


def nt(a, b):
    return lax.dot_general(a, b, (((1,), (1,)), ((), ())), preferred_element_type=FULL)


def tn(a, b):
    return lax.dot_general(a, b, (((0,), (0,)), ((), ())), preferred_element_type=FULL)


def rows_at(block, size):
    return pl.ds(pl.multiple_of(block * size, size), size)


def call(kernel, name, outs, table, *args, scratch=(), flops=0, nbytes=0):
    return pl.pallas_call(
        kernel,
        name=name,
        out_shape=[jax.ShapeDtypeStruct(shape, dtype) for shape, dtype in outs],
        in_specs=[SMEM] + [VMEM] * len(args),
        out_specs=[VMEM] * len(outs),
        scratch_shapes=[pltpu.VMEM(shape, dtype) for shape, dtype in scratch],
        cost_estimate=pl.CostEstimate(
            flops=0, bytes_accessed=0, transcendentals=0
        ),
    )(table, *args)


def attend_kernel(parts, table, t0, t1, t2, t3, *refs):
    pieces, refs = refs[:parts], refs[parts:]
    tok, w, wm, vec, qp, kp, v, q_t, k_t, o_t, lse, keep, send, heads, v_t = refs
    seq, y = table[0], table[1]
    rows = t0.shape[0]
    width = w.shape[0]
    piece = width // parts
    length = tok.shape[0]
    for j, t in enumerate((t0, t1, t2, t3)):
        tok[rows_at(seq ^ j, rows), :] = t[...]
    total = jnp.zeros(vec.shape, FULL)
    for p, ref in enumerate(pieces):
        at = rows_at(table[4 + p], piece)
        w[at, :] = ref[:piece, :640]
        wm[at, :] = ref[:piece, 640:]
        total = total + ref[piece : piece + HEADER, :].astype(FULL)
    vec[...] = total
    bias = vec[8:9, :640]
    lane = lax.broadcasted_iota(jnp.int32, (rows, 256), 1)
    mark = (lane - 192).astype(FULL)
    for i in range(length // rows):
        here = slice(i * rows, (i + 1) * rows)
        x = nn(tok[here, :width], w[...]) + bias
        seg = tok[here, width : width + 128].astype(FULL)
        seg = jnp.concatenate([seg, seg], axis=1)
        q = x[:, :256].astype(LOW).astype(FULL) * 0.125
        q = jnp.where(lane < 192, q, jnp.where((lane < 196) & (mark != seg), FAR, 0.0))
        k = pltpu.roll(x[:, 128:384], 192, 1).astype(LOW).astype(FULL)
        k = jnp.where(lane < 192, k, jnp.where(mark == seg, 1.0, 0.0))
        vv = x[:, 384:640]
        qp[here, :] = q.astype(LOW)
        kp[here, :] = k.astype(LOW)
        v[here, :] = vv.astype(LOW)
        q_t[:, here] = q.T.astype(LOW)
        k_t[:, here] = k.T.astype(LOW)
        v_t[:, here] = vv.T.astype(LOW)
        for h in range(3):
            heads[h, here, :] = jnp.where(
                (lane // HEAD_DIM == h) | (lane >= 192), k, 0.0
            ).astype(LOW)
    lse[...] = jnp.zeros(lse.shape, FULL)

    @pl.loop(0, length // 256)
    def _(i):
        cols = rows_at(i, 256)
        for h in range(3):
            mine = slice(HEAD_DIM * h, HEAD_DIM * (h + 1))
            scores = nn(heads[h], q_t[:, cols])
            top = jnp.max(scores, axis=0, keepdims=True)
            expo = jnp.exp(scores - top)
            total = jnp.sum(expo, axis=0, keepdims=True)
            mixed = nn(v_t[mine, :], expo.astype(LOW))
            o_t[mine, cols] = mixed * (1.0 / total)
            lse[h : h + 1, cols] = top + jnp.log(total)

    half = length // 2
    keep[...] = o_t[:, rows_at(y, half)].astype(LOW)
    send[...] = o_t[:, rows_at(1 - y, half)].astype(LOW)


def gelu_parts(u):
    phi = 0.5 + 0.5 * lax.erf(u * 0.7071067811865476)
    bell = jnp.exp(-0.5 * u * u)
    return u * phi, phi + u * (bell * 0.3989422804014327)


def merge_kernel(table, a0, a1, a2, a3, tok, vec, mine, theirs, att, normed, rstd, low, bias, work):
    seq, y, c = table[0], table[1], table[2]
    count, width = normed.shape
    half = width // 2
    for j, a in enumerate((a0, a1, a2, a3)):
        att[rows_at(seq ^ j, 192), :] = a[...]
    bias[...] = jnp.broadcast_to(
        jnp.concatenate([vec[6:7, :width], vec[7:8, :width]], axis=1), bias.shape
    )
    work[:, rows_at(c, half)] = tn(att[...], mine[...])
    work[:, rows_at(1 - c, half)] = tn(att[...], theirs[...])
    values = tok[rows_at(y, count), :width].astype(FULL) + work[...] + vec[0:1, :width]
    center = values - jnp.mean(values, axis=1, keepdims=True)
    scale = lax.rsqrt(jnp.mean(center * center, axis=1, keepdims=True) + 1e-12)
    center = center * scale
    normed[...] = center
    rstd[...] = jnp.broadcast_to(scale, rstd.shape)
    low[...] = (center * vec[1:2, :width] + vec[2:3, :width]).astype(LOW)


def gelu_kernel(parts, table, low, bias, *refs):
    pieces, (e, act, slope) = refs[:parts], refs[parts:]
    piece = e.shape[0] // parts
    for p, ref in enumerate(pieces):
        e[rows_at(table[4 + p], piece), :] = ref[...]

    @pl.loop(0, act.shape[1] // 256)
    def _(i):
        cols = rows_at(i, 256)
        pre = nn(low[...], e[:, cols]) + bias[0:1, cols]
        value, grad = gelu_parts(pre)
        act[:, cols] = value.astype(LOW)
        slope[:, cols] = grad.astype(LOW)


def shrink_kernel(parts, table, act, *refs):
    pieces, (sh, part) = refs[:parts], refs[parts:]
    piece = sh.shape[0] // parts
    for p, ref in enumerate(pieces):
        sh[rows_at(table[4 + p], piece), :] = ref[...]
    part[...] = nn(act[...], sh[...]).astype(LOW)


def second_kernel(table, normed, vec, mine, theirs, cot_mine, cot_theirs, *refs):
    out, dsec, dz, sums, work = refs
    c = table[2]
    rows = cot_mine.shape[0]
    width = normed.shape[1]
    first = normed[...] * vec[1:2, :width] + vec[2:3, :width]
    second = first + (mine[...].astype(FULL) + theirs[...].astype(FULL)) + vec[3:4, :width]
    center = second - jnp.mean(second, axis=1, keepdims=True)
    scale = lax.rsqrt(jnp.mean(center * center, axis=1, keepdims=True) + 1e-12)
    center = center * scale
    gain = vec[4:5, :width]
    work[...] = center * gain + vec[5:6, :width]
    out[...] = work[rows_at(c, rows), :].astype(LOW)
    work[rows_at(c, rows), :] = cot_mine[...].astype(FULL)
    work[rows_at(1 - c, rows), :] = cot_theirs[...].astype(FULL)
    up = work[...]
    sums[...] = jnp.zeros(sums.shape, FULL)
    sums[0:1, :] = jnp.sum(up * center, axis=0, keepdims=True)
    sums[1:2, :] = jnp.sum(up, axis=0, keepdims=True)
    scaled = up * gain
    grad = scale * (
        scaled
        - jnp.mean(scaled, axis=1, keepdims=True)
        - center * jnp.mean(scaled * center, axis=1, keepdims=True)
    )
    dsec[...] = grad
    dz[...] = grad.astype(LOW)
    sums[2:3, :] = jnp.sum(dz[...].astype(FULL), axis=0, keepdims=True)


def hidden_kernel(table, dz, slope, e, sh, dpre, dfp, sums):
    hidden = sh.shape[0]
    sums[...] = jnp.zeros(sums.shape, FULL)

    @pl.loop(0, hidden // 256)
    def _(i):
        cols = rows_at(i, 256)
        value = nt(dz[...], sh[cols, :]) * slope[:, cols].astype(FULL)
        value = value.astype(LOW)
        dpre[:, cols] = value
        sums[0:1, cols] = jnp.sum(value.astype(FULL), axis=0, keepdims=True)

    dfp[...] = nt(dpre[...], e[...]).astype(LOW)


def put_blocks(parts, table, work, block, outs, extra=None):
    for i, ref in enumerate(outs):
        for j in range(parts // len(outs)):
            at = table[4 + parts + i * (parts // len(outs)) + j]
            ref[j, :block, :] = work[rows_at(at, block), :]
            if extra is not None:
                ref[j, block:, :] = extra


def shrink_grad_kernel(parts, table, act, dz, *refs):
    outs, work = refs[:4], refs[4]
    work[...] = tn(act[...], dz[...]).astype(LOW)
    put_blocks(parts, table, work, work.shape[0] // parts, outs)


def first_kernel(
    table, mine, theirs, dsec, normed, rstd, vec, wm, wm_other, dres, dbr, dkeep, dsend, sums, work
):
    seq, c = table[0], table[2]
    width = normed.shape[1]
    half = width // 2
    rows = dres.shape[0]
    up = (mine[...].astype(FULL) + theirs[...].astype(FULL)) + dsec[...]
    center = normed[...]
    sums[...] = jnp.zeros(sums.shape, FULL)
    sums[0:1, :] = jnp.sum(up * center, axis=0, keepdims=True)
    sums[1:2, :] = jnp.sum(up, axis=0, keepdims=True)
    scaled = up * vec[1:2, :width]
    work[...] = rstd[:, 0:1] * (
        scaled
        - jnp.mean(scaled, axis=1, keepdims=True)
        - center * jnp.mean(scaled * center, axis=1, keepdims=True)
    )
    dbr[...] = work[...].astype(LOW)
    dres[...] = work[rows_at(c, rows), :]
    sums[2:3, :] = jnp.sum(dbr[...].astype(FULL), axis=0, keepdims=True)
    for j, ref in ((0, dkeep), (2, dsend)):
        at = rows_at(seq ^ j, 192)
        ref[...] = (
            nt(wm[at, :], dbr[:, rows_at(c, half)])
            + nt(wm_other[at, :], dbr[:, rows_at(1 - c, half)])
        ).astype(LOW)


def expand_grad_kernel(parts, table, low, dpre, att, dbr, sums_two, sums_hid, sums_one, *refs):
    outs, (work, rows) = refs[:4], refs[4:]
    c = table[2]
    width = low.shape[1]
    half = width // 2
    work[:, :half] = nn(att[...], dbr[:, rows_at(c, half)]).astype(LOW)
    work[:, half:] = tn(low[...], dpre[...]).astype(LOW)
    rows[...] = jnp.zeros(rows.shape, FULL)
    rows[0:1, :width] = sums_one[2:3, :]
    rows[1:3, :width] = sums_one[0:2, :]
    rows[3:4, :width] = sums_two[2:3, :]
    rows[4:6, :width] = sums_two[0:2, :]
    rows[6:7, : dpre.shape[1]] = sums_hid[0:1, :]
    put_blocks(parts, table, work, width // parts, outs, rows[...].astype(LOW))


def attend_back_kernel(
    parts, table, tok, qp, kp, v, q_t, k_t, o_t, lse, dkeep, dother, *refs
):
    outs, refs = refs[:2], refs[2:]
    grads, probs, dscores, d_t, d_rows, q_rows, heads, v_heads, dq_t, work = refs
    y = table[1]
    length = tok.shape[0]
    width = work.shape[0]
    block = width // parts
    half = length // 2
    d_t[192:, :] = jnp.zeros((64, length), LOW)
    d_t[:192, rows_at(y, half)] = dkeep[...]
    d_t[:192, rows_at(1 - y, half)] = dother[...]
    lane = lax.broadcasted_iota(jnp.int32, (256, 256), 1)
    for i in range(length // 256):
        here = slice(i * 256, (i + 1) * 256)
        d = d_t[:, here].astype(FULL).T
        k = kp[here, :].astype(FULL)
        q = qp[here, :].astype(FULL)
        vv = v[here, :].astype(FULL)
        for h in range(3):
            own = lane // HEAD_DIM == h
            at = slice(h * length + i * 256, h * length + (i + 1) * 256)
            d_rows[at, :] = jnp.where(own, d, 0.0).astype(LOW)
            q_rows[at, :] = jnp.where(own, q, 0.0).astype(LOW)
            heads[h, here, :] = jnp.where(own | (lane >= 192), k, 0.0).astype(LOW)
            v_heads[h, here, :] = jnp.where(own, vv, 0.0).astype(LOW)
    dq_t[192:, :] = jnp.zeros((64, length), FULL)

    @pl.loop(0, length // 256)
    def _(i):
        cols = rows_at(i, 256)
        for h in range(3):
            mine = slice(HEAD_DIM * h, HEAD_DIM * (h + 1))
            out = pl.ds(pl.multiple_of(h * length + i * 256, 256), 256)
            prob = jnp.exp(nn(heads[h], q_t[:, cols]) - lse[h : h + 1, cols])
            probs[:, out] = prob.astype(LOW)
            delta = jnp.sum(
                d_t[mine, cols].astype(FULL) * o_t[mine, cols], axis=0, keepdims=True
            )
            grad = (prob * (nn(v_heads[h], d_t[:, cols]) - delta)).astype(LOW)
            dscores[:, out] = grad
            dq_t[mine, cols] = nn(k_t[mine, :], grad) * 0.125

    for i in range(length // 256):
        here = slice(i * 256, (i + 1) * 256)
        dv = nn(probs[here, :], d_rows[...])
        dk = pltpu.roll(nn(dscores[here, :], q_rows[...]), 192, 1)
        dq = dq_t[:, here].T
        grads[here, :256] = jnp.where(lane < 192, dq, dk).astype(LOW)
        grads[here, 256:384] = dk[:, :128].astype(LOW)
        grads[here, 384:] = dv.astype(LOW)
    work[...] = tn(tok[:, :width], grads[...]).astype(LOW)
    total = jnp.sum(grads[...].astype(FULL), axis=0, keepdims=True)
    total = jnp.broadcast_to(total, (EXTRA, total.shape[1])).astype(LOW)
    put_blocks(parts, table, work, block, outs, total)


def input_grad_kernel(table, grads, w, send, keep, work):
    seq = table[0]
    rows = send.shape[1]
    work[...] = nt(grads[...], w[...]).astype(LOW)
    for b in range(2):
        send[b] = work[rows_at(seq ^ (1 + 2 * b), rows), :]
        keep[b] = work[rows_at(seq ^ (2 * b), rows), :]


def pair_kernel(keep, got, *outs):
    for k, ref in enumerate(outs):
        ref[...] = (keep[k].astype(FULL) + got[k].astype(FULL)).astype(LOW)


def projection_kernel(table, wq, wk, wv, merge, rest, out):
    seq, c = table[0], table[2]
    share, width = wq.shape
    slim, half = width // 4, width // 2
    for s in range(4):

        @pl.when(seq == s)
        def _():
            cols = slice(slim * s, slim * (s + 1))
            for i, ref in enumerate((wq, wk, wv)):
                out[:share, slim * i : slim * (i + 1)] = ref[:, cols]

    out[:share, 3 * slim : 640] = jnp.zeros((share, 640 - 3 * slim), LOW)
    out[:share, 640:] = merge[:, rows_at(c, half)]
    out[share:, :] = rest[...]


def wide_kernel(unit, table, wide, out):
    c = table[2]
    for s in range(2):

        @pl.when(c == s)
        def _():
            for f in range(out.shape[1] // unit):
                start = 2 * unit * f + unit * s
                out[:, unit * f : unit * (f + 1)] = wide[:, start : start + unit]


def final_projection_kernel(table, p0, p1, p2, p3, dq, dk, dv, rows, stack):
    seq = table[0]
    share = dq.shape[0]
    slim = dq.shape[1] // 4
    for j, p in enumerate((p0, p1, p2, p3)):
        stack[j] = p[...].astype(FULL)
    for i in range(4):
        part = stack[seq ^ i]
        cols = slice(slim * i, slim * (i + 1))
        for g, ref in enumerate((dq, dk, dv)):
            ref[:, cols] = part[:share, slim * g : slim * (g + 1)]
            if g != 1:
                rows[4 * g : 4 * g + 8, cols] = part[share : share + 8, slim * g : slim * (g + 1)]


def final_wide_kernel(table, mine, theirs, merge, wide, rows, both):
    c = table[2]
    share, half = merge.shape[0], merge.shape[1] // 2
    hidden = wide.shape[1]
    unit = hidden // 16
    both[c] = mine[...]
    both[1 - c] = theirs[...]
    for s in range(2):
        merge[:, half * s : half * (s + 1)] = both[s, :share, :half]
        for f in range(8):
            start = half + unit * f
            at = 2 * unit * f + unit * s
            wide[:, at : at + unit] = both[s, :share, start : start + unit]
        rows[s] = both[s, share:, :]


def after(x, *others):
    return lax.optimization_barrier((x,) + others)[0]


class Link:
    def __init__(self, window=2):
        self.window = window
        self.done = []

    def send(self, x, axis, pairs, *others, free=False):
        if len(self.done) >= self.window and not free:
            others = others + (self.done[-self.window],)
        if others:
            x = after(x, *others)
        self.done.append(lax.ppermute(x, axis, pairs))
        return self.done[-1]


NEAR_PAIRS = [(i, i ^ 1) for i in range(8)]
SHIFTS = {k: [(i, (i + 2 * k) % 8) for i in range(8)] for k in (1, 2, 3)}


def swap_core(x):
    return lax.ppermute(x, "seq", CORE_PAIRS)


def gather_whole(shard, count, extra):
    whole = lax.all_gather(shard, "fsdp", axis=0)
    rows = shard.shape[0] - extra
    main = whole[:, :rows].reshape(count * rows, shard.shape[1])
    if not extra:
        return [main]
    rest = jnp.sum(whole[:, rows:].astype(FULL), axis=0).astype(LOW)
    return [jnp.concatenate([main, rest], axis=0)]


def scatter_whole(send, keep, count, extra):
    both = jnp.concatenate([send, keep], axis=0)
    rows = both.shape[1] - extra
    main = both[:, :rows].reshape(count, -1, both.shape[2])
    rest = jnp.broadcast_to(both[:1, rows:], (count, extra, both.shape[2]))
    both = jnp.concatenate([main, rest], axis=1)
    return lax.psum_scatter(both, "fsdp", scatter_dimension=0).astype(FULL)


def pair_sum(keep, got):
    shape = keep.shape[1:]
    return pl.pallas_call(
        pair_kernel,
        name="pair",
        out_shape=[jax.ShapeDtypeStruct(shape, LOW)] * keep.shape[0],
        in_specs=[VMEM, VMEM],
        out_specs=[VMEM] * keep.shape[0],
        cost_estimate=pl.CostEstimate(
            flops=0, bytes_accessed=0, transcendentals=0
        ),
    )(keep, got)


def body(
    count,
    tokens,
    segment_ids,
    query_weight,
    key_weight,
    value_weight,
    merge_weight,
    query_bias,
    value_bias,
    merge_bias,
    first_gain,
    first_shift,
    expand_weight,
    expand_bias,
    shrink_weight,
    shrink_bias,
    second_gain,
    second_shift,
    cotangent,
):
    rows, width = tokens.shape[1:]
    hidden = expand_weight.shape[1]
    share = width // count
    unit = hidden // count // 2
    slim = width // 4
    half = width // 2
    length = 4 * rows
    near_rows = 2 * rows
    seq = lax.axis_index("seq")
    own = lax.axis_index("fsdp")
    c, y = seq % 2, seq // 2
    z, x = own // 2, own % 2
    ring = count == 8
    if ring:
        parts = parts_in = 8
        mine = [((z - k) % 4) * 2 + x for k in (0, 1, 3, 2)]
        pieces = mine + [2 * (m // 2) + 1 - x for m in mine]
        there = [2 * ((z + k) % 4) for k in (2, 1, 3, 0)]
        blocks = [t + 1 - x for t in there] + [t + x for t in there]
    else:
        parts, parts_in = 4, 1
        pieces, blocks = [0], [0, 1, 2, 3]
    pieces = pieces + [0] * (parts - parts_in)
    table = jnp.stack([seq, y, c, z] + pieces + blocks).astype(jnp.int32)
    x_link, y_link, z_link = Link(), Link(), Link()

    def near(v, *others, free=False):
        return x_link.send(v, "fsdp", NEAR_PAIRS, *others, free=free)

    def along(v, k, *others, free=False):
        return z_link.send(v, "fsdp", SHIFTS[k], *others, free=free)

    def across(v, *others):
        return y_link.send(v, "seq", CHIP_PAIRS, *others)

    pair = jnp.stack([query_bias, value_bias])
    pair = lax.dynamic_update_slice(jnp.zeros((2, width), LOW), pair, (0, share * own))
    pair = lax.dynamic_slice(pair, (0, slim * seq), (2, slim))
    bias_row = jnp.concatenate([pair[0:1], jnp.zeros((1, slim), LOW), pair[1:2]], axis=1)
    rest = jnp.zeros((HEADER, 640 + half), LOW)
    stack = jnp.stack(
        [merge_bias, first_gain, first_shift, shrink_bias, second_gain, second_shift]
    )
    rest = lax.dynamic_update_slice(rest, stack, (0, share * own))
    chunk = lax.dynamic_slice(expand_bias, (unit * c,), (unit,)).reshape(1, unit)
    rest = lax.dynamic_update_slice(
        rest, chunk, (6 + unit * own // width, unit * own % width)
    )
    rest = lax.dynamic_update_slice(rest, bias_row, (8, 0))
    (shard,) = call(
        projection_kernel,
        "projection",
        [((share + HEADER, 640 + half), LOW)],
        table,
        query_weight,
        key_weight,
        value_weight,
        merge_weight,
        rest,
    )
    inputs = tokens.reshape(rows, width)
    marks = jnp.broadcast_to(segment_ids.reshape(rows, 1).astype(LOW), (rows, 128))

    def wide_shard(dep):
        weight = after(expand_weight, dep)
        if ring:
            return call(
                partial(wide_kernel, unit),
                "wide",
                [((share, hidden // 2), LOW)],
                table,
                weight,
            )[0]
        wide = weight.reshape(share, count, 2, unit)
        return jnp.where(c == 0, wide[:, :, 0], wide[:, :, 1]).reshape(share, hidden // 2)

    low_shard = lax.dynamic_slice(shrink_weight, (unit * c, 0), (unit, width))
    if ring:
        q1 = along(shard, 1)
        q3 = along(shard, 3)
        q2 = along(shard, 2)
        qx0 = near(shard)
        inputs = jnp.concatenate([inputs, marks], axis=1)
        t_two = across(inputs)
        t_one = swap_core(inputs)
        qx1 = near(q1)
        e0 = wide_shard(q1)
        ex0 = near(e0)
        qx3 = near(q3)
        qx2 = near(q2)
        w_pieces = [shard, q1, q3, q2, qx0, qx1, qx3, qx2]
        t_three = swap_core(t_two)
        e1 = along(e0, 1)
        e3 = along(e0, 3)
        ex1 = near(e1)
        s0 = after(low_shard, q3)
        sx0 = near(s0)
        e2 = along(e0, 2)
        w_pieces[-1] = after(qx2, e1)
    else:
        w_pieces = gather_whole(shard, count, HEADER)
        inputs = jnp.concatenate([inputs, marks], axis=1)
        t_two = across(inputs)
        t_one = swap_core(inputs)
        t_three = swap_core(t_two)
        e_pieces = gather_whole(wide_shard(shard), count, 0)
        sh_pieces = gather_whole(low_shard, count, 0)

    tok, w, wm, vec, qp, kp, v, q_t, k_t, o_t, lse, keep, send = call(
        partial(attend_kernel, parts_in),
        "attend",
        [
            ((length, width + 128), LOW),
            ((width, 640), LOW),
            ((width, half), LOW),
            ((HEADER, 640 + half), FULL),
            ((length, 256), LOW),
            ((length, 256), LOW),
            ((length, 256), LOW),
            ((256, length), LOW),
            ((256, length), LOW),
            ((slim, length), FULL),
            ((8, length), FULL),
            ((slim, near_rows), LOW),
            ((slim, near_rows), LOW),
        ],
        table,
        inputs,
        t_one,
        t_two,
        t_three,
        *w_pieces,
        scratch=[((3, length, 256), LOW), ((256, length), LOW)],
        flops=14e9,
        nbytes=1e7,
    )
    a_two = across(send)
    a_one = swap_core(keep)
    wm_other = swap_core(wm)
    a_three = swap_core(a_two)
    cot = cotangent.reshape(rows, width)
    cot_other = swap_core(after(cot, keep))
    if ring:
        ex3 = near(e3, keep)
        s1 = along(s0, 1, keep)
        ex2 = near(e2)
        s3 = along(s0, 3)
        s2 = along(s0, 2)
        sx1 = near(s1)
        sx3 = near(s3)
        sx2 = near(s2)
        e_pieces = [e0, e1, e3, e2, ex0, ex1, ex3, ex2]
        sh_pieces = [s0, s1, s3, s2, sx0, sx1, sx3, sx2]

    att, normed, rstd, low, e_bias = call(
        merge_kernel,
        "merge",
        [
            ((width, near_rows), LOW),
            ((near_rows, width), FULL),
            ((near_rows, 128), FULL),
            ((near_rows, width), LOW),
            ((EXTRA, hidden // 2), FULL),
        ],
        table,
        keep,
        a_one,
        a_two,
        a_three,
        tok,
        vec,
        wm,
        wm_other,
        scratch=[((near_rows, width), FULL)],
        flops=5e9,
        nbytes=1e7,
    )
    if ring:
        e_pieces[-1] = after(e_pieces[-1], low)
    e, act, slope = call(
        partial(gelu_kernel, parts_in),
        "gelu",
        [
            ((width, hidden // 2), LOW),
            ((near_rows, hidden // 2), LOW),
            ((near_rows, hidden // 2), LOW),
        ],
        table,
        low,
        e_bias,
        *e_pieces,
        flops=8e9,
        nbytes=1e7,
    )
    sh, part = call(
        partial(shrink_kernel, parts_in),
        "shrink",
        [((hidden // 2, width), LOW), ((near_rows, width), LOW)],
        table,
        act,
        *sh_pieces,
        flops=4e9,
        nbytes=1e7,
    )
    part_other = swap_core(part)
    out, dsec, dz, sums_two = call(
        second_kernel,
        "second",
        [
            ((rows, width), LOW),
            ((near_rows, width), FULL),
            ((near_rows, width), LOW),
            ((EXTRA, width), FULL),
        ],
        table,
        normed,
        vec,
        part,
        part_other,
        cot,
        cot_other,
        scratch=[((near_rows, width), FULL)],
        flops=5e9,
        nbytes=8e6,
    )
    sh_blocks = call(
        partial(shrink_grad_kernel, parts),
        "shrink_grad",
        [((parts // 4, hidden // 2 // parts, width), LOW)] * 4,
        table,
        act,
        dz,
        scratch=[((hidden // 2, width), LOW)],
        flops=5e9,
        nbytes=5e6,
    )
    dpre, dfp, sums_hid = call(
        hidden_kernel,
        "hidden",
        [
            ((near_rows, hidden // 2), LOW),
            ((near_rows, width), LOW),
            ((EXTRA, hidden // 2), FULL),
        ],
        table,
        after(dz, sh_blocks[0]),
        slope,
        e,
        sh,
        flops=6e9,
        nbytes=8e6,
    )
    dfp_other = swap_core(dfp)
    dres, dbr, dkeep, dsend, sums_one = call(
        first_kernel,
        "first",
        [
            ((rows, width), FULL),
            ((near_rows, width), LOW),
            ((slim, near_rows), LOW),
            ((slim, near_rows), LOW),
            ((EXTRA, width), FULL),
        ],
        table,
        dfp,
        dfp_other,
        dsec,
        normed,
        rstd,
        vec,
        wm,
        wm_other,
        scratch=[((near_rows, width), FULL)],
        flops=5e9,
        nbytes=8e6,
    )
    dother = across(dsend)
    em_blocks = call(
        partial(expand_grad_kernel, parts),
        "expand_grad",
        [((parts // 4, width // parts + EXTRA, half + hidden // 2), LOW)] * 4,
        table,
        low,
        dpre,
        att,
        dbr,
        sums_two,
        sums_hid,
        sums_one,
        scratch=[((width, half + hidden // 2), LOW), ((EXTRA, half + hidden // 2), FULL)],
        flops=5e9,
        nbytes=8e6,
    )
    def finish_half(blocks, got, i):
        if i == 0:
            p2, p1 = pair_sum(blocks[2], got)
            return along(p2, 2, free=True), along(p1, 1, free=True), p1
        p3, p0 = pair_sum(blocks[3], got)
        return along(p3, 3, free=True), p0

    if ring:
        sh_got = [near(sh_blocks[0], free=True), near(sh_blocks[1], free=True)]
        em_got = [near(em_blocks[0], sh_got[0], free=True)]
        r2, r1, mark = finish_half(sh_blocks, after(sh_got[0], em_blocks[0]), 0)
        sh_sums = [r2, r1]
        gate = mark
    else:
        gate = em_blocks[0]
    *w_blocks, grads = call(
        partial(attend_back_kernel, parts),
        "attend_back",
        [((parts // 2, width // parts + EXTRA, 640), LOW)] * 2 + [((length, 640), LOW)],
        table,
        tok,
        qp,
        kp,
        v,
        q_t,
        k_t,
        o_t,
        lse,
        dkeep,
        after(dother, gate),
        scratch=[
            ((length, 3 * length), LOW),
            ((length, 3 * length), LOW),
            ((256, length), LOW),
            ((3 * length, 256), LOW),
            ((3 * length, 256), LOW),
            ((3, length, 256), LOW),
            ((3, length, 256), LOW),
            ((256, length), FULL),
            ((width, 640), LOW),
        ],
        flops=16e9,
        nbytes=1e7,
    )
    if ring:
        sh_sums += list(finish_half(sh_blocks, after(sh_got[1], grads, r1, r2), 1))
        gate = sh_sums[-1]
    else:
        gate = w_blocks[0]
    x_send, x_keep = call(
        input_grad_kernel,
        "input_grad",
        [((2, rows, width), LOW)] * 2,
        table,
        after(grads, gate),
        w,
        scratch=[((length, width), LOW)],
        flops=4e9,
        nbytes=5e6,
    )
    x_sum = x_keep.astype(FULL) + swap_core(x_send).astype(FULL)
    x_other = across(x_sum[1].astype(LOW))
    in_grad = dres + x_sum[0] + x_other.astype(FULL)


    if ring:
        em_got.append(near(em_blocks[1], grads, free=True))
        r2, r1, mark = finish_half(em_blocks, after(em_got[0], x_send), 0)
        em_sums = [r2, r1]
        w_got = near(w_blocks[0], em_got[1], free=True)
        em_sums += list(finish_half(em_blocks, after(em_got[1], mark), 1))
        mark = em_sums[-1]
        sh_sums[-1] = after(sh_sums[-1], mark)
        p2, p1, p3, p0 = pair_sum(w_blocks[1], after(w_got, mark))
        w_sums = [along(p, k, free=True) for p, k in ((p2, 2), (p1, 1), (p3, 3))] + [p0]
        shrink_own, em_own, w_own = [
            g[0].astype(FULL) + g[1].astype(FULL) + g[2].astype(FULL) + g[3].astype(FULL)
            for g in (sh_sums, em_sums, w_sums)
        ]
    else:
        shrink_own, em_own, w_own = [
            scatter_whole(
                jnp.concatenate(g[: len(g) // 2], axis=0), jnp.concatenate(g[len(g) // 2 :], axis=0), count, extra
            )
            for g, extra in ((sh_blocks, 0), (em_blocks, EXTRA), (w_blocks, EXTRA))
        ]
    w_own = w_own.astype(LOW)

    def over_chips(part):
        part = part.astype(LOW)
        return part.astype(FULL) + across(part).astype(FULL)

    def both_cores(part):
        other = swap_core(part)
        return jnp.where(c == 0, part, other), jnp.where(c == 0, other, part)

    sh_low, sh_high = both_cores(over_chips(shrink_own))
    d_shrink = jnp.concatenate([sh_low, sh_high], axis=0)
    em_own = over_chips(em_own)
    w_two = across(w_own)
    w_one = swap_core(w_own)
    w_three = swap_core(w_two)
    em_other = swap_core(em_own)
    d_merge, d_expand, em_rows = final_wide(
        ring, table, c, em_own, em_other, share, half, hidden, unit, count
    )
    small = lax.dynamic_slice(em_rows[0], (0, share * own), (6, share))
    d_b_expand = jnp.concatenate(
        [
            lax.dynamic_slice(em_rows[i], (6, unit * own), (1, unit)).reshape(unit)
            for i in range(2)
        ]
    )
    d_q, d_k, d_v, w_rows = call(
        final_projection_kernel,
        "final_projection",
        [((share, width), FULL)] * 3 + [((16, width), FULL)],
        table,
        w_own,
        w_one,
        w_two,
        w_three,
        scratch=[((4, share + EXTRA, 640), FULL)],
    )
    w_rows = lax.dynamic_slice(w_rows, (0, share * own), (16, share))

    return (
        out.reshape(1, rows, width),
        in_grad.astype(LOW).reshape(1, rows, width),
        d_q,
        d_k,
        d_v,
        d_merge,
        w_rows[0],
        w_rows[8],
        small[0],
        small[1],
        small[2],
        d_expand,
        d_b_expand,
        d_shrink,
        small[3],
        small[4],
        small[5],
    )


def final_wide(ring, table, c, mine, theirs, share, half, hidden, unit, count):
    if ring:
        return call(
            final_wide_kernel,
            "final_wide",
            [
                ((share, 2 * half), FULL),
                ((share, hidden), FULL),
                ((2, EXTRA, half + hidden // 2), FULL),
            ],
            table,
            mine,
            theirs,
            scratch=[((2, share + EXTRA, half + hidden // 2), FULL)],
        )
    low, high = jnp.where(c == 0, mine, theirs), jnp.where(c == 0, theirs, mine)
    merge = jnp.concatenate([low[:share, :half], high[:share, :half]], axis=1)
    wide = jnp.stack(
        [part[:share, half:].reshape(share, count, unit) for part in (low, high)], axis=2
    ).reshape(share, hidden)
    return merge, wide, jnp.stack([low[share:], high[share:]])


def solution(mesh):
    row, flat = P("fsdp", None), P("fsdp")
    cube = P("fsdp", "seq", None)
    return jax.shard_map(
        partial(body, mesh.shape["fsdp"]),
        mesh=mesh,
        in_specs=(cube, P("fsdp", "seq"))
        + (row,) * 4
        + (flat,) * 5
        + (row, flat, row)
        + (flat,) * 3
        + (cube,),
        out_specs=(cube, cube) + (row,) * 4 + (flat,) * 5 + (row, flat, row) + (flat,) * 3,
        check_vma=False,
    )
```
